128 devices in a mesh: grp: 8 (over z, core), dom: 16 (over y, x).
Axes of the slice: x: 4, y: 4, z: 4, core: 2. Of those that a mesh axis runs over, the one named last changes fastest.
Arguments:
- parent_local: float32 [8192, 296], P(('grp', 'dom')), may hold values from -6 to 6
- parent_slot: int32 [65536], P(('grp', 'dom')), may hold values from 0 to 79, as said below
- child_octant: int32 [65536], P(('grp', 'dom')), may hold values from 0 to 7
- child_m2l: float32 [65536, 296], P(('grp', 'dom')), may hold values from -6 to 6
- l2l_ops: float32 [8, 296, 296], replicated, may hold values from -0.375 to 0.375
- leaf_center: float32 [65536, 3], P(('grp', 'dom')), may hold values from 0 to 2
- src_coords: float32 [65536, 3, 128], P(('grp', 'dom')), may hold values from 0 to 2
- src_charge: float32 [65536, 128], P(('grp', 'dom')), may hold values from -6 to 6
- obs_owner: int32 [65536], replicated, may hold values from 0 to 127, as said below
- obs_offset: float32 [131072, 3, 128], P(('grp', 'dom')), may hold values from -1 to 1
- near_slots: int32 [131072, 8], P(('grp', 'dom')), may hold values from 0 to 1023, as said below
Outputs:
- leaf_local: float32 [65536, 296], P(('grp', 'dom'))
- potential: float32 [131072, 128], P(('grp', 'dom'))
The draws below stay inside these ranges and needn't reach their ends.
Inputs may be any that keep to these rules, and one draw needn't show every extreme that they name: `parent_slot`: values below 16 name the last 16 parents of the previous device in the flat order over grp and dom; a value v of 16 or more names the device's own parent v - 16. Nondecreasing within a device; the first device names only its own parents. `obs_owner`: among one device's 512 leaves at most 8 share an owner; one owner receives exactly 8 leaves from every device. `near_slots`: the first entry of a row is the row's own index within its device; the others are rows of the same device that hold a leaf.
All inputs are finite; a program needn't handle non-finite values.
Results may differ from the reference program's by a relative error of at most 0.0003.
Values sent between devices are 32-bit elements; how exact they have to be, the bound alone decides.
A program may use at most 64 MiB of HBM per device.

```python
import math
import jax
import jax.numpy as jnp
import numpy as np
from jax import lax

ORDER = 8
Q = 296
BLK = 128
NEAR = 8
RIM = 16
LEAF_DEV = 512
PAR_DEV = 64
LEAVES = 65536
PARENTS = 8192
SLOTS = 1024
OBS_ROWS = 131072
N_GRP = 8
N_DOM = 16


def owner_table(key):
    device_list = N_GRP * N_DOM
    capacity = 2 * LEAF_DEV // device_list
    slot_table = device_list * capacity
    busiest_owner = jax.random.randint(jax.random.fold_in(key, 101), (), 0, device_list)
    frequent_owners = jax.random.randint(jax.random.fold_in(key, 102), (device_list,), 0, 4) == 0
    target_owner = jnp.arange(slot_table, dtype=jnp.int32) // capacity
    extra_weight = jnp.where(frequent_owners[target_owner], 8192, 0) + jnp.where(target_owner == busiest_owner, 32768, 0)
    owner_scores = jax.random.randint(jax.random.fold_in(key, 103), (device_list, slot_table), 0, 16384) + extra_weight[None, :]
    distinct = owner_scores * slot_table + jnp.arange(slot_table, dtype=jnp.int32)[None, :]
    chosen = lax.top_k(distinct, LEAF_DEV)[1]
    owners = target_owner[chosen]
    shuffle_keys = jax.random.split(jax.random.fold_in(key, 104), device_list)
    orders = jax.vmap(lambda sub_key: jax.random.permutation(sub_key, LEAF_DEV))(shuffle_keys)
    return jnp.take_along_axis(owners, orders, axis=1).astype(jnp.int32)


def draw_obs_owner(key, part):
    return owner_table(key).reshape(-1)


def draw_near_slots(key, part):
    device_list = N_GRP * N_DOM
    capacity = 2 * LEAF_DEV // device_list
    slot_table = device_list * capacity
    owners = owner_table(key)
    counts = jnp.sum((owners[:, :, None] == jnp.arange(device_list, dtype=jnp.int32)[None, None, :]).astype(jnp.int32), axis=1)
    live_rows = (jnp.arange(capacity, dtype=jnp.int32)[None, None, :] < counts.T[:, :, None]).reshape(device_list, slot_table)
    live_count = jnp.maximum(jnp.sum(live_rows.astype(jnp.int32), axis=1), 1)
    owner_scores = jax.random.randint(jax.random.fold_in(key, 201), (device_list, slot_table), 0, 4096) + live_rows.astype(jnp.int32) * 4096
    distinct = owner_scores * slot_table + jnp.arange(slot_table, dtype=jnp.int32)[None, :]
    ordered = lax.top_k(distinct, slot_table)[1]
    picks = jax.random.randint(jax.random.fold_in(key, 202), (device_list, slot_table, NEAR - 1), 0, live_count[:, None, None])
    others = jax.vmap(lambda order_row, pick_rows: order_row[pick_rows])(ordered, picks)
    selves = jnp.broadcast_to(jnp.arange(slot_table, dtype=jnp.int32)[None, :, None], (device_list, slot_table, 1))
    return jnp.concatenate([selves, others.astype(jnp.int32)], axis=2).reshape(device_list * slot_table, NEAR)


def draw_parent_slot(key, part):
    device_list = N_GRP * N_DOM
    window = RIM + LEAF_DEV // 8
    raw_slots = jax.random.randint(jax.random.fold_in(key, 301), (device_list, LEAF_DEV), 0, window)
    lowest = jnp.where(jnp.arange(device_list, dtype=jnp.int32) == 0, RIM, 0)
    raw_slots = jnp.maximum(raw_slots, lowest[:, None])
    ordered = jnp.sort(raw_slots, axis=1)
    ordered = ordered.at[:, LEAF_DEV - 1].set(window - 1)
    ordered = ordered.at[:, 0].set(lowest)
    return ordered.reshape(-1).astype(jnp.int32)


def touch_ends(entries, own_key, least, top_value):
    dims = entries.shape
    index_at = [jax.random.randint(jax.random.fold_in(own_key, axis), (), 0, dims[axis]) for axis in range(len(dims))]
    entries = entries.at[tuple(index_at)].set(least)
    longest = dims.index(max(dims))
    index_at[longest] = (index_at[longest] + 1) % dims[longest]
    return entries.at[tuple(index_at)].set(top_value)


def levels(rng, dims, cuts, low, high):
    factor_of = 1.0
    for axis_at, shards_of in cuts:
        heights = jax.random.uniform(jax.random.fold_in(jax.random.fold_in(rng, 6), axis_at), (shards_of,), jnp.float32, low / len(cuts), high / len(cuts))
        factor_of = factor_of * jnp.repeat(jnp.exp(heights), dims[axis_at] // shards_of).reshape((-1,) + (1,) * (len(dims) - 1 - axis_at))
    return factor_of


def scatter_about(rng, dims, deviation, limit, shards=(), kind=jnp.bfloat16):
    entries = jax.random.normal(rng, dims, jnp.float32) * deviation
    if len(shards) > 0:
        entries = levels(rng, dims, shards, -0.22, 0.18) * entries
    return jnp.clip(entries, min=-limit, max=limit).astype(kind)


def setup_inputs(seed: int = 0) -> dict:
    keys = jax.random.split(jax.random.key(seed), 12)
    return {
        "parent_local": scatter_about(keys[0], (PARENTS, Q), 1.0, 6.0, ((0, 128),), jnp.float32),
        "parent_slot": draw_parent_slot(jax.random.fold_in(keys[11], 71), 0),
        "child_octant": touch_ends(jax.random.randint(keys[2], (LEAVES,), 0, 8), jax.random.fold_in(keys[2], 1), 0, 7).astype(jnp.int32),
        "child_m2l": scatter_about(keys[3], (LEAVES, Q), 1.0, 6.0, ((0, 128),), jnp.float32),
        "l2l_ops": scatter_about(keys[4], (8, Q, Q), Q ** -0.5, 0.375, (), jnp.float32),
        "leaf_center": jnp.clip(2.0 * jax.random.uniform(keys[5], (LEAVES, 3), jnp.float32) ** levels(keys[5], (LEAVES, 3), ((0, 128),), -0.2, 0.2), 0.0, 2.0),
        "src_coords": jnp.clip(2.0 * jax.random.uniform(keys[6], (LEAVES, 3, BLK), jnp.float32) ** levels(keys[6], (LEAVES, 3, BLK), ((0, 128),), -0.2, 0.2), 0.0, 2.0),
        "src_charge": scatter_about(keys[7], (LEAVES, BLK), 1.0, 6.0, ((0, 128),), jnp.float32),
        "obs_owner": draw_obs_owner(jax.random.fold_in(keys[11], 71), 0),
        "obs_offset": jnp.clip(jax.random.uniform(keys[9], (OBS_ROWS, 3, BLK), jnp.float32, -1.0, 1.0) * levels(keys[9], (OBS_ROWS, 3, BLK), ((0, 128),), -0.4, 0.0), -1.0, 1.0),
        "near_slots": draw_near_slots(jax.random.fold_in(keys[11], 71), 0),
    }


RADIUS = 2.95
half_width = 0.5
soft_sq = 0.0025
four_pi = 4.0 * math.pi

def surface_points():
    grid = np.linspace(-1.0, 1.0, ORDER)
    points = np.stack(np.meshgrid(grid, grid, grid, indexing='ij'), 0).reshape(3, -1)
    on_surface = np.max(np.abs(points), axis=0) > 1.0 - 1e-09
    return jnp.asarray(points[:, on_surface] * RADIUS, dtype=jnp.float32)

def far_block(densities, offsets):
    surface = surface_points()
    dist_sq = jnp.zeros((offsets.shape[0], surface.shape[1], offsets.shape[2]), jnp.float32)
    for component in range(3):
        separation = offsets[:, component, None, :] - surface[component][None, :, None]
        dist_sq = dist_sq + separation * separation
    kernel = 1.0 / (four_pi * half_width * jnp.sqrt(dist_sq))
    return jnp.einsum('sq,sqb->sb', densities, kernel, precision=lax.Precision.HIGHEST)

def near_block(targets, fetch_rows, neighbours):
    summed = jnp.zeros((targets.shape[0], targets.shape[2]), jnp.float32)
    for column in range(neighbours.shape[1]):
        coords, charges = fetch_rows(neighbours[:, column])
        dist_sq = jnp.full((targets.shape[0], targets.shape[2], coords.shape[2]), soft_sq, jnp.float32)
        for component in range(3):
            separation = targets[:, component, :, None] - coords[:, component, None, :]
            dist_sq = dist_sq + separation * separation
        summed = summed + lax.optimization_barrier(jnp.sum(charges[:, None, :] * lax.rsqrt(dist_sq), axis=2))
    return summed / four_pi

def reference(parent_local, parent_slot, child_octant, child_m2l, l2l_ops, leaf_center, src_coords, src_charge, obs_owner, obs_offset, near_slots):
    device_list = N_GRP * N_DOM
    capacity = SLOTS // device_list
    leaf_index = jnp.arange(LEAVES, dtype=jnp.int32)
    source_dev = leaf_index // LEAF_DEV
    parent_global = source_dev * PAR_DEV + parent_slot - RIM
    moved = jnp.einsum('pr,oqr->opq', parent_local, l2l_ops, precision=lax.Precision.HIGHEST)
    stacked = moved.reshape(8 * PARENTS, Q)
    leaf_local = child_m2l + stacked[(child_octant * PARENTS + parent_global).astype(jnp.int32)]
    owners = obs_owner.reshape(device_list, LEAF_DEV)
    onehot = (owners[:, :, None] == jnp.arange(device_list, dtype=jnp.int32)[None, None, :]).astype(jnp.int32)
    before = jnp.cumsum(onehot, axis=1) - onehot
    leaf_rank = lax.optimization_barrier(jnp.sum(before * onehot, axis=2)).reshape(LEAVES)
    slot_row = (obs_owner * SLOTS + source_dev * capacity + leaf_rank).astype(jnp.int32)
    slot_leaf = jnp.full((OBS_ROWS,), -1, jnp.int32).at[slot_row].set(leaf_index)
    receiver = jnp.arange(OBS_ROWS, dtype=jnp.int32) // SLOTS
    near_leaf = slot_leaf[(near_slots + receiver[:, None] * SLOTS).astype(jnp.int32)]

    def fetch_rows(leaves):
        is_live = leaves >= 0
        clipped = jnp.maximum(leaves, 0)
        return (src_coords[clipped], jnp.where(is_live[:, None], src_charge[clipped], 0.0))

    def one_block(pieces):
        block_leaf, offsets, block_near = pieces
        is_live = block_leaf >= 0
        clipped = jnp.maximum(block_leaf, 0)
        densities = jnp.where(is_live[:, None], leaf_local[clipped], 0.0)
        centers = leaf_center[clipped]
        targets = centers[:, :, None] + half_width * offsets
        far_part = far_block(densities, offsets)
        near_part = near_block(targets, fetch_rows, block_near)
        return jnp.where(is_live[:, None], far_part + near_part, 0.0)
    blocks = OBS_ROWS // 64
    potential = lax.map(one_block, (slot_leaf.reshape(blocks, 64), obs_offset.reshape(blocks, 64, 3, BLK), near_leaf.reshape(blocks, 64, NEAR)))
    return (leaf_local, potential.reshape(OBS_ROWS, BLK))
```

```python
import functools
import math

import jax
import jax.numpy as jnp
import numpy as np
from jax import lax
from jax.experimental import pallas as pl
from jax.experimental.pallas import tpu as pltpu
from jax.sharding import PartitionSpec as P

ORDER = 8
RIM = 16
RADIUS = 2.95
HALF = 0.5
SOFT_SQ = 0.0025
AXES = ("grp", "dom")
F32 = jnp.float32
BF16 = jnp.bfloat16
FEATURES = 32


def from_behind(block, axis, distance):
    devices = range(lax.axis_size(axis))
    route = [(i - distance, i) for i in devices if i - distance in devices]
    return lax.ppermute(block, axis, route)


def pack_kernel(capacity, owner, coords, charge, center, out, dest, count, tail):
    devices = out.shape[0]
    leaves = coords.shape[0]
    out[...] = jnp.zeros_like(out)
    tail[:, 0:3] = center[...]
    tail[:, 3:4] = jnp.ones((leaves, 1), F32)

    def clear(i, carry):
        count[i] = 0
        return carry

    lax.fori_loop(0, devices, clear, 0, unroll=8)

    def place(j, carry):
        o = owner[j]
        rank = count[o]
        count[o] = rank + 1
        dest[j] = o * capacity + rank
        row = coords[j]
        for c in range(3):
            out[o, c, pl.ds(rank, 1), :] = row[c : c + 1]
        out[o, 3, pl.ds(rank, 1), :] = charge[pl.ds(j, 1), :]
        out[o, 4, pl.ds(rank, 1), 0:4] = tail[pl.ds(j, 1), :]
        return carry

    lax.fori_loop(0, leaves, place, 0, unroll=4)


def pack(owner, coords, charge, center, devices, capacity):
    leaves = coords.shape[0]
    vmem = pl.BlockSpec(memory_space=pltpu.VMEM)
    return pl.pallas_call(
        functools.partial(pack_kernel, capacity),
        out_shape=(
            jax.ShapeDtypeStruct((devices, 5, capacity, 128), F32),
            jax.ShapeDtypeStruct((leaves,), jnp.int32),
        ),
        in_specs=[pl.BlockSpec(memory_space=pltpu.SMEM), vmem, vmem, vmem],
        out_specs=(vmem, pl.BlockSpec(memory_space=pltpu.SMEM)),
        scratch_shapes=[pltpu.SMEM((devices,), jnp.int32), pltpu.VMEM((leaves, 4), F32)],
        compiler_params=pltpu.CompilerParams(vmem_limit_bytes=24 << 20),
        name="pack",
    )(owner, coords, charge, center)


def leaf_kernel(which, dest, stacked, m2l, leaf, dens):
    leaves = m2l.shape[0]
    dens[...] = jnp.zeros_like(dens)

    def place(j, carry):
        row = m2l[pl.ds(j, 1), :] + stacked[pl.ds(which[j], 1), :]
        leaf[pl.ds(j, 1), :] = row
        dens[pl.ds(dest[j], 1), :] = row
        return carry

    lax.fori_loop(0, leaves, place, 0, unroll=8)


def leaf_rows(which, dest, stacked, m2l, slots):
    width = m2l.shape[1]
    vmem = pl.BlockSpec(memory_space=pltpu.VMEM)
    smem = pl.BlockSpec(memory_space=pltpu.SMEM)
    return pl.pallas_call(
        leaf_kernel,
        out_shape=(
            jax.ShapeDtypeStruct(m2l.shape, F32),
            jax.ShapeDtypeStruct((slots, width), F32),
        ),
        in_specs=[smem, smem, vmem, vmem],
        out_specs=(vmem, vmem),
        compiler_params=pltpu.CompilerParams(vmem_limit_bytes=24 << 20),
        name="leaf_rows",
    )(which, dest, stacked, m2l)


def split3(v):
    high = v.astype(BF16).astype(F32)
    rest = v - high
    middle = rest.astype(BF16).astype(F32)
    return high, middle, rest - middle


def target_features(x, y, z):
    out = []
    for v in (x, y, z):
        h, m, l = split3(v)
        out += [h, h, h, m, m, l]
    return out + list(split3(x * x + y * y + z * z + SOFT_SQ))


def source_features(x, y, z):
    out = []
    for v in (x, y, z):
        h, m, l = split3(-2.0 * v)
        out += [h, m, l, h, m, h]
    return out, list(split3(x * x + y * y + z * z))


def near_kernel(group, unroll, near_list, src, off, out, table, charges, tfeat, sfeat):
    step = pl.program_id(0)
    senders, _, cap, _ = src.shape
    ones = jnp.ones((8, 128), F32)
    zeros = jnp.zeros((8, 128), F32)

    @pl.when(step == 0)
    def _():
        for f in range(18, 21):
            sfeat[8 * f : 8 * f + 8] = ones
        for f in range(24, FEATURES):
            sfeat[8 * f : 8 * f + 8] = zeros
        for u in range(unroll):
            for f in range(21, 24):
                tfeat[u, 8 * f : 8 * f + 8] = ones
            for f in range(24, FEATURES):
                tfeat[u, 8 * f : 8 * f + 8] = zeros

        def prepare(i, carry):
            cross, square = source_features(*(src[i, c] - 1.0 for c in range(3)))
            for f, v in list(enumerate(cross)) + list(enumerate(square, 21)):
                sfeat[8 * f : 8 * f + 8] = v
            for s in range(8):
                table[i * 8 + s] = sfeat[pl.ds(s, FEATURES, stride=8), :].astype(BF16)
            charges[pl.ds(i * 8, 8)] = src[i, 3] * (0.25 / math.pi)
            return carry

        lax.fori_loop(0, senders, prepare, 0)

    lane_part = lax.broadcasted_iota(jnp.int32, (128, 128), 1) // FEATURES

    def rows(i, carry):
        for u in range(unroll):
            local = i * unroll + u
            block = step * group + local
            info = src[block, 4]
            shift = off[local]
            place = [(info[:, c : c + 1] - 1.0) + HALF * shift[:, c] for c in range(3)]
            for f, v in enumerate(target_features(*place)):
                tfeat[u, 8 * f : 8 * f + 8] = v
            for s in range(8):
                feat = tfeat[u, pl.ds(s, FEATURES, stride=8), :]
                turned = jnp.concatenate([feat.astype(BF16)] * 4, axis=0).T
                left = jnp.concatenate(
                    [jnp.where(lane_part == k, turned, jnp.zeros_like(turned)) for k in range(4)],
                    axis=0,
                )
                at = [near_list[(block * 8 + s) * 8 + j] for j in range(8)]
                right = jnp.concatenate(
                    [
                        jnp.concatenate([table[at[2 * k]], table[at[2 * k + 1]]], axis=1)
                        for k in range(4)
                    ],
                    axis=0,
                )
                dist_sq = jnp.dot(left, right, preferred_element_type=F32)
                total = None
                for k in range(4):
                    for h in range(2):
                        weight = charges[pl.ds(at[2 * k + h], 1), :]
                        part = dist_sq[128 * k : 128 * k + 128, 128 * h : 128 * h + 128]
                        term = lax.rsqrt(part) * weight
                        total = term if total is None else total + term
                out[pl.ds(local * 8 + s, 1), :] = jnp.sum(total.T, axis=0, keepdims=True)
            live = info[:, 3:4] > 0.5
            out[pl.ds(local * 8, 8), :] = jnp.where(live, out[pl.ds(local * 8, 8), :], 0.0)
        return carry

    lax.fori_loop(0, group // unroll, rows, 0)


def near_field(src, offsets, near_slots, group=16, unroll=2):
    senders, _, cap, _ = src.shape
    slots = senders * cap
    return pl.pallas_call(
        functools.partial(near_kernel, group, unroll),
        out_shape=jax.ShapeDtypeStruct((slots, 128), F32),
        grid_spec=pltpu.PrefetchScalarGridSpec(
            num_scalar_prefetch=1,
            grid=(senders // group,),
            in_specs=[
                pl.BlockSpec(src.shape, lambda g, n: (0, 0, 0, 0)),
                pl.BlockSpec((group, cap, 3, 128), lambda g, n: (g, 0, 0, 0)),
            ],
            out_specs=pl.BlockSpec((group * cap, 128), lambda g, n: (g, 0)),
            scratch_shapes=[
                pltpu.VMEM((slots, FEATURES, 128), BF16),
                pltpu.VMEM((slots, 128), F32),
                pltpu.VMEM((unroll, FEATURES * 8, 128), F32),
                pltpu.VMEM((FEATURES * 8, 128), F32),
            ],
        ),
        compiler_params=pltpu.CompilerParams(vmem_limit_bytes=40 << 20),
        cost_estimate=pl.CostEstimate(
            flops=2 * slots * 512 * 128 * 256, bytes_accessed=8 << 20, transcendentals=slots << 17
        ),
        name="near_field",
    )(near_slots, src, offsets)


def far_kernel(dens, off, near, out):
    grid = [float(v) for v in (np.linspace(-1.0, 1.0, ORDER) * RADIUS).astype(np.float32)]
    edge = (0, ORDER - 1)

    def block(i, carry):
        shift = off[i]
        axis_sq = []
        for c in range(3):
            o = shift[:, c]
            axis_sq.append([(o - v) * (o - v) for v in grid])
        weights = dens[pl.ds(i * 8, 8), :]
        sums = [None] * 4
        q = 0
        for a in range(ORDER):
            for b in range(ORDER):
                plane = axis_sq[0][a] + axis_sq[1][b]
                last = range(ORDER) if a in edge or b in edge else edge
                for c in last:
                    term = weights[:, q : q + 1] * lax.rsqrt(plane + axis_sq[2][c])
                    sums[q % 4] = term if sums[q % 4] is None else sums[q % 4] + term
                    q += 1
        total = (sums[0] + sums[1]) + (sums[2] + sums[3])
        out[pl.ds(i * 8, 8), :] = near[pl.ds(i * 8, 8), :] + total * (0.25 / (math.pi * HALF))
        return carry

    lax.fori_loop(0, off.shape[0], block, 0)


def far_field(dens, offsets, near, group=32):
    senders, cap, _, points = offsets.shape
    slots, width = dens.shape
    return pl.pallas_call(
        far_kernel,
        out_shape=jax.ShapeDtypeStruct((slots, points), F32),
        grid=(senders // group,),
        in_specs=[
            pl.BlockSpec((group * cap, width), lambda g: (g, 0)),
            pl.BlockSpec((group, cap, 3, points), lambda g: (g, 0, 0, 0)),
            pl.BlockSpec((group * cap, points), lambda g: (g, 0)),
        ],
        out_specs=pl.BlockSpec((group * cap, points), lambda g: (g, 0)),
        cost_estimate=pl.CostEstimate(
            flops=4 * slots * points * width,
            bytes_accessed=4 << 20,
            transcendentals=slots * points * width,
        ),
        name="far_field",
    )(dens, offsets, near)


def on_device(
    parent_local,
    parent_slot,
    child_octant,
    child_m2l,
    l2l_ops,
    leaf_center,
    src_coords,
    src_charge,
    obs_owner,
    obs_offset,
    near_slots,
):
    devices = lax.axis_size(AXES)
    leaf_dev, width = child_m2l.shape
    slots, _, points = obs_offset.shape
    cap = slots // devices
    me = lax.axis_index(AXES)
    mine = lax.dynamic_slice_in_dim(obs_owner, me * leaf_dev, leaf_dev)

    packed, dest = pack(mine, src_coords, src_charge, leaf_center, devices, cap)
    received = lax.all_to_all(packed, AXES, 0, 0, tiled=True)

    rim = from_behind(parent_local[parent_local.shape[0] - RIM :], AXES, 1)
    parents = jnp.concatenate([rim, parent_local], axis=0)
    moved = jnp.einsum("pr,oqr->opq", parents, l2l_ops, precision=lax.Precision.HIGHEST)
    stacked = moved.reshape(l2l_ops.shape[0] * parents.shape[0], width)
    which = child_octant * parents.shape[0] + parent_slot
    leaf_local, dens = leaf_rows(which, dest, stacked, child_m2l, slots)
    dens = lax.all_to_all(dens.reshape(devices, cap, width), AXES, 0, 0, tiled=True)

    offsets = obs_offset.reshape(devices, cap, 3, points)
    near = near_field(received, offsets, near_slots.reshape(-1))
    potential = far_field(dens.reshape(slots, width), offsets, near)
    return (leaf_local, potential)


def solution(mesh):
    placed = (
        P(AXES, None),
        P(AXES),
        P(AXES),
        P(AXES, None),
        P(),
        P(AXES, None),
        P(AXES, None, None),
        P(AXES, None),
        P(),
        P(AXES, None, None),
        P(AXES, None),
    )
    return jax.shard_map(
        on_device,
        mesh=mesh,
        in_specs=placed,
        out_specs=(P(AXES, None), P(AXES, None)),
        check_vma=False,
    )
```

```python
import functools
import math

import jax
import jax.numpy as jnp
import ml_dtypes
import numpy as np
from jax import lax
from jax.experimental import pallas as pl
from jax.experimental.pallas import tpu as pltpu
from jax.sharding import PartitionSpec as P

ORDER = 8
RIM = 16
RADIUS = 2.95
HALF = 0.5
SOFT_SQ = 0.0025
AXES = ("grp", "dom")
F32 = jnp.float32
BF16 = jnp.bfloat16
FEATURES = 32


def from_behind(block, axis, distance):
    devices = range(lax.axis_size(axis))
    route = [(i - distance, i) for i in devices if i - distance in devices]
    return lax.ppermute(block, axis, route)


def pack_kernel(capacity, owner, coords, charge, center, out, dest, count, tail):
    devices = out.shape[0]
    leaves = coords.shape[0]
    out[...] = jnp.zeros_like(out)
    tail[:, 0:3] = center[...]
    tail[:, 3:4] = jnp.ones((leaves, 1), F32)

    def clear(i, carry):
        count[i] = 0
        return carry

    lax.fori_loop(0, devices, clear, 0, unroll=8)

    def place(j, carry):
        o = owner[j]
        rank = count[o]
        count[o] = rank + 1
        dest[j] = o * capacity + rank
        row = coords[j]
        for c in range(3):
            out[o, c, pl.ds(rank, 1), :] = row[c : c + 1]
        out[o, 3, pl.ds(rank, 1), :] = charge[pl.ds(j, 1), :]
        out[o, 4, pl.ds(rank, 1), 0:4] = tail[pl.ds(j, 1), :]
        return carry

    lax.fori_loop(0, leaves, place, 0, unroll=4)


def pack(owner, coords, charge, center, devices, capacity):
    leaves = coords.shape[0]
    vmem = pl.BlockSpec(memory_space=pltpu.VMEM)
    return pl.pallas_call(
        functools.partial(pack_kernel, capacity),
        out_shape=(
            jax.ShapeDtypeStruct((devices, 5, capacity, 128), F32),
            jax.ShapeDtypeStruct((leaves,), jnp.int32),
        ),
        in_specs=[pl.BlockSpec(memory_space=pltpu.SMEM), vmem, vmem, vmem],
        out_specs=(vmem, pl.BlockSpec(memory_space=pltpu.SMEM)),
        scratch_shapes=[pltpu.SMEM((devices,), jnp.int32), pltpu.VMEM((leaves, 4), F32)],
        compiler_params=pltpu.CompilerParams(vmem_limit_bytes=24 << 20),
        name="pack",
    )(owner, coords, charge, center)


def leaf_kernel(which, stacked, m2l, leaf, dens):
    leaves, width = m2l.shape
    dens[...] = jnp.zeros_like(dens)

    def place(j, carry):
        row = m2l[pl.ds(j, 1), :] + stacked[pl.ds(which[j], 1), :]
        leaf[pl.ds(j, 1), :] = row
        dens[pl.ds(j, 1), 0:width] = row
        return carry

    lax.fori_loop(0, leaves, place, 0, unroll=8)


def leaf_rows(which, stacked, m2l, padded):
    vmem = pl.BlockSpec(memory_space=pltpu.VMEM)
    smem = pl.BlockSpec(memory_space=pltpu.SMEM)
    return pl.pallas_call(
        leaf_kernel,
        out_shape=(
            jax.ShapeDtypeStruct(m2l.shape, F32),
            jax.ShapeDtypeStruct((m2l.shape[0], padded), F32),
        ),
        in_specs=[smem, vmem, vmem],
        out_specs=(vmem, vmem),
        compiler_params=pltpu.CompilerParams(vmem_limit_bytes=24 << 20),
        cost_estimate=pl.CostEstimate(flops=1 << 18, bytes_accessed=8 << 20, transcendentals=0),
        name="leaf_rows",
    )(which, stacked, m2l)


def split3(v):
    high = v.astype(BF16).astype(F32)
    rest = v - high
    middle = rest.astype(BF16).astype(F32)
    return high, middle, rest - middle


def target_features(x, y, z, extra):
    out = []
    for v in (x, y, z):
        h, m, l = split3(v)
        out += [h, h, h, m, m, l]
    return out + list(split3(x * x + y * y + z * z + extra))


def source_features(x, y, z):
    out = []
    for v in (x, y, z):
        h, m, l = split3(-2.0 * v)
        out += [h, m, l, h, m, h]
    return out, list(split3(x * x + y * y + z * z))


def near_kernel(group, unroll, near_list, src, off, out, table, charges, tfeat, sfeat):
    step = pl.program_id(0)
    senders, _, cap, _ = src.shape
    ones = jnp.ones((8, 128), F32)
    zeros = jnp.zeros((8, 128), F32)

    @pl.when(step == 0)
    def _():
        for f in range(18, 21):
            sfeat[8 * f : 8 * f + 8] = ones
        for f in range(24, FEATURES):
            sfeat[8 * f : 8 * f + 8] = zeros
        for u in range(unroll):
            for f in range(21, 24):
                tfeat[u, 8 * f : 8 * f + 8] = ones
            for f in range(24, FEATURES):
                tfeat[u, 8 * f : 8 * f + 8] = zeros

        def prepare(i, carry):
            cross, square = source_features(*(src[i, c] - 1.0 for c in range(3)))
            for f, v in list(enumerate(cross)) + list(enumerate(square, 21)):
                sfeat[8 * f : 8 * f + 8] = v
            for s in range(8):
                table[i * 8 + s] = sfeat[pl.ds(s, FEATURES, stride=8), :].astype(BF16)
            charges[pl.ds(i * 8, 8)] = src[i, 3] * (0.25 / math.pi)
            return carry

        lax.fori_loop(0, senders, prepare, 0)

    lane_part = lax.broadcasted_iota(jnp.int32, (128, 128), 1) // FEATURES

    def rows(i, carry):
        for u in range(unroll):
            local = i * unroll + u
            block = step * group + local
            info = src[block, 4]
            place = [
                (info[:, c : c + 1] - 1.0) + HALF * off[c, pl.ds(local * 8, 8), :] for c in range(3)
            ]
            for f, v in enumerate(target_features(*place, SOFT_SQ)):
                tfeat[u, 8 * f : 8 * f + 8] = v
            for s in range(8):
                feat = tfeat[u, pl.ds(s, FEATURES, stride=8), :]
                turned = jnp.concatenate([feat.astype(BF16)] * 4, axis=0).T
                left = jnp.concatenate(
                    [jnp.where(lane_part == k, turned, jnp.zeros_like(turned)) for k in range(4)],
                    axis=0,
                )
                at = [near_list[(block * 8 + s) * 8 + j] for j in range(8)]
                right = jnp.concatenate(
                    [
                        jnp.concatenate([table[at[2 * k]], table[at[2 * k + 1]]], axis=1)
                        for k in range(4)
                    ],
                    axis=0,
                )
                dist_sq = jnp.dot(left, right, preferred_element_type=F32)
                total = None
                for k in range(4):
                    for h in range(2):
                        weight = charges[pl.ds(at[2 * k + h], 1), :]
                        part = dist_sq[128 * k : 128 * k + 128, 128 * h : 128 * h + 128]
                        term = lax.rsqrt(part) * weight
                        total = term if total is None else total + term
                out[pl.ds(local * 8 + s, 1), :] = jnp.sum(total.T, axis=0, keepdims=True)
            live = info[:, 3:4] > 0.5
            out[pl.ds(local * 8, 8), :] = jnp.where(live, out[pl.ds(local * 8, 8), :], 0.0)
        return carry

    lax.fori_loop(0, group // unroll, rows, 0)


def near_field(src, offsets, near_slots, group=16, unroll=4):
    senders, _, cap, _ = src.shape
    slots = senders * cap
    return pl.pallas_call(
        functools.partial(near_kernel, group, unroll),
        out_shape=jax.ShapeDtypeStruct((slots, 128), F32),
        grid_spec=pltpu.PrefetchScalarGridSpec(
            num_scalar_prefetch=1,
            grid=(senders // group,),
            in_specs=[
                pl.BlockSpec(src.shape, lambda g, n: (0, 0, 0, 0)),
                pl.BlockSpec((3, group * cap, 128), lambda g, n: (0, g, 0)),
            ],
            out_specs=pl.BlockSpec((group * cap, 128), lambda g, n: (g, 0)),
            scratch_shapes=[
                pltpu.VMEM((slots, FEATURES, 128), BF16),
                pltpu.VMEM((slots, 128), F32),
                pltpu.VMEM((unroll, FEATURES * 8, 128), F32),
                pltpu.VMEM((FEATURES * 8, 128), F32),
            ],
        ),
        compiler_params=pltpu.CompilerParams(vmem_limit_bytes=40 << 20),
        cost_estimate=pl.CostEstimate(
            flops=2 * slots * 512 * 128 * 256, bytes_accessed=8 << 20, transcendentals=slots << 17
        ),
        name="near_field",
    )(near_slots, src, offsets)


def surface_weights():
    grid = np.linspace(-1.0, 1.0, ORDER)
    points = np.stack(np.meshgrid(grid, grid, grid, indexing="ij"), 0).reshape(3, -1)
    on_surface = np.max(np.abs(points), axis=0) > 1.0 - 1e-09
    points = (points[:, on_surface] * RADIUS).astype(np.float32)
    fill = 320 - points.shape[1]
    points = np.concatenate([points, np.repeat(points[:, :1], fill, axis=1)], axis=1)

    def split(v):
        high = v.astype(ml_dtypes.bfloat16).astype(np.float32)
        rest = v - high
        middle = rest.astype(ml_dtypes.bfloat16).astype(np.float32)
        return high, middle, rest - middle

    rows = []
    for c in range(3):
        h, m, l = split(-2.0 * points[c])
        rows += [h, m, l, h, m, h]
    rows += [np.ones(320, np.float32)] * 3
    rows += list(split(np.sum(points * points, axis=0)))
    rows += [np.zeros(320, np.float32)] * (FEATURES - len(rows))
    rows = np.stack(rows)
    main = np.repeat(rows[:, :256], 8, axis=0)
    last = np.zeros((FEATURES, 8, 512), np.float32)
    for s in range(8):
        last[:, s, 64 * s : 64 * s + 64] = rows[:, 256:]
    last = last.reshape(FEATURES * 8, 512)
    return main.astype(ml_dtypes.bfloat16), last.astype(ml_dtypes.bfloat16)


def far_kernel(unroll, dest, off, dens, main, last, out, tfeat, shift):
    ones = jnp.ones((8, 128), F32)
    zeros = jnp.zeros((8, 128), F32)
    out[...] = jnp.zeros_like(out)
    for u in range(unroll):
        for f in range(21, 24):
            tfeat[u, 8 * f : 8 * f + 8] = ones
        for f in range(24, FEATURES):
            tfeat[u, 8 * f : 8 * f + 8] = zeros
    row_of_lane = lax.broadcasted_iota(jnp.int32, (128, 8 * FEATURES), 1) % 8
    low_half = lax.broadcasted_iota(jnp.int32, (1, 128), 1) < 64

    def rows(i, carry):
        for u in range(unroll):
            first = (i * unroll + u) * 8
            at = [dest[first + t] for t in range(8)]
            for t in range(8):
                for c in range(3):
                    shift[u, c, t : t + 1, :] = off[at[t] // 8, c, pl.ds(at[t] % 8, 1), :]
            for f, v in enumerate(target_features(*(shift[u, c] for c in range(3)), 0.0)):
                tfeat[u, 8 * f : 8 * f + 8] = v
            turned = tfeat[u].astype(BF16).T
            weights = [dens[pl.ds(first + t, 1), :] for t in range(8)]
            tail_sq = jnp.dot(turned, last[...], preferred_element_type=F32)
            for p in range(4):
                pair = jnp.where(
                    low_half,
                    weights[2 * p][:, 256:384],
                    pltpu.roll(weights[2 * p + 1][:, 256:384], 64, 1),
                )
                tail = lax.rsqrt(tail_sq[:, 128 * p : 128 * p + 128]) * pair
                for h in range(2):
                    t = 2 * p + h
                    left = jnp.where(row_of_lane == t, turned, jnp.zeros_like(turned))
                    dist_sq = jnp.dot(left, main[...], preferred_element_type=F32)
                    total = lax.rsqrt(dist_sq[:, :128]) * weights[t][:, :128]
                    total = total + lax.rsqrt(dist_sq[:, 128:]) * weights[t][:, 128:256]
                    total = total + jnp.where(low_half == (h == 0), tail, 0.0)
                    line = jnp.sum(total.T, axis=0, keepdims=True)
                    out[pl.ds(at[t], 1), :] = line * (0.25 / (math.pi * HALF))
        return carry

    lax.fori_loop(0, dens.shape[0] // (8 * unroll), rows, 0)


def far_field(dest, offsets, dens, unroll=4):
    devices, _, cap, points = offsets.shape
    main, last = surface_weights()
    vmem = pl.BlockSpec(memory_space=pltpu.VMEM)
    return pl.pallas_call(
        functools.partial(far_kernel, unroll),
        out_shape=jax.ShapeDtypeStruct((devices * cap, points), F32),
        in_specs=[pl.BlockSpec(memory_space=pltpu.SMEM)] + [vmem] * 4,
        out_specs=vmem,
        scratch_shapes=[
            pltpu.VMEM((unroll, FEATURES * 8, 128), F32),
            pltpu.VMEM((unroll, 3, 8, 128), F32),
        ],
        compiler_params=pltpu.CompilerParams(vmem_limit_bytes=24 << 20),
        cost_estimate=pl.CostEstimate(
            flops=2 * dens.shape[0] * 128 * 256 * 384,
            bytes_accessed=4 << 20,
            transcendentals=dens.shape[0] * 128 * 320,
        ),
        name="far_field",
    )(dest, offsets, dens, jnp.asarray(main), jnp.asarray(last))


def on_device(
    parent_local,
    parent_slot,
    child_octant,
    child_m2l,
    l2l_ops,
    leaf_center,
    src_coords,
    src_charge,
    obs_owner,
    obs_offset,
    near_slots,
):
    devices = lax.axis_size(AXES)
    leaf_dev, width = child_m2l.shape
    slots, _, points = obs_offset.shape
    cap = slots // devices
    me = lax.axis_index(AXES)
    mine = lax.dynamic_slice_in_dim(obs_owner, me * leaf_dev, leaf_dev)

    rim = from_behind(parent_local[parent_local.shape[0] - RIM :], AXES, 1)
    packed, dest = pack(mine, src_coords, src_charge, leaf_center, devices, cap)

    offsets = jnp.transpose(obs_offset, (1, 0, 2))
    outgoing = jnp.transpose(offsets.reshape(3, devices, cap, points), (1, 0, 2, 3))
    outgoing, rim = lax.optimization_barrier((outgoing, rim))
    at_leaves = lax.all_to_all(outgoing, AXES, 0, 0, tiled=True)
    received = lax.all_to_all(packed, AXES, 0, 0, tiled=True)

    parents = jnp.concatenate([rim, parent_local], axis=0)
    moved = jnp.einsum("pr,oqr->opq", parents, l2l_ops, precision=lax.Precision.HIGHEST)
    stacked = moved.reshape(l2l_ops.shape[0] * parents.shape[0], width)
    which = child_octant * parents.shape[0] + parent_slot
    leaf_local, dens = leaf_rows(which, stacked, child_m2l, 384)
    far = far_field(dest, at_leaves, dens)
    received, far = lax.optimization_barrier((received, far))
    far = lax.all_to_all(far.reshape(devices, cap, points), AXES, 0, 0, tiled=True)

    near = near_field(received, offsets, near_slots.reshape(-1))
    return (leaf_local, near + far.reshape(slots, points))


def solution(mesh):
    placed = (
        P(AXES, None),
        P(AXES),
        P(AXES),
        P(AXES, None),
        P(),
        P(AXES, None),
        P(AXES, None, None),
        P(AXES, None),
        P(),
        P(AXES, None, None),
        P(AXES, None),
    )
    return jax.shard_map(
        on_device,
        mesh=mesh,
        in_specs=placed,
        out_specs=(P(AXES, None), P(AXES, None)),
        check_vma=False,
    )
```

```python
import functools
import math

import jax
import jax.numpy as jnp
import ml_dtypes
import numpy as np
from jax import lax
from jax.experimental import pallas as pl
from jax.experimental.pallas import tpu as pltpu
from jax.sharding import PartitionSpec as P

ORDER = 8
RIM = 16
RADIUS = 2.95
HALF = 0.5
SOFT_SQ = 0.0025
AXES = ("grp", "dom")
F32 = jnp.float32
BF16 = jnp.bfloat16
FEATURES = 32


def from_behind(block, axis, distance):
    devices = range(lax.axis_size(axis))
    route = [(i - distance, i) for i in devices if i - distance in devices]
    return lax.ppermute(block, axis, route)


def pack_kernel(capacity, owner, coords, charge, center, out, dest, count, tail):
    devices = out.shape[0]
    leaves = charge.shape[0]
    out[...] = jnp.zeros_like(out)
    tail[:, 0:3] = center[...]
    tail[:, 3:4] = jnp.ones((leaves, 1), F32)

    def clear(i, carry):
        count[i] = 0
        return carry

    lax.fori_loop(0, devices, clear, 0, unroll=8)

    def place(j, carry):
        o = owner[j]
        rank = count[o]
        count[o] = rank + 1
        dest[j] = o * capacity + rank
        for c in range(3):
            out[o, c, pl.ds(rank, 1), :] = coords[c, pl.ds(j, 1), :]
        out[o, 3, pl.ds(rank, 1), :] = charge[pl.ds(j, 1), :]
        out[o, 4, pl.ds(rank, 1), 0:4] = tail[pl.ds(j, 1), :]
        return carry

    lax.fori_loop(0, leaves, place, 0, unroll=4)


def pack(owner, coords, charge, center, devices, capacity):
    leaves = charge.shape[0]
    vmem = pl.BlockSpec(memory_space=pltpu.VMEM)
    return pl.pallas_call(
        functools.partial(pack_kernel, capacity),
        out_shape=(
            jax.ShapeDtypeStruct((devices, 5, capacity, 128), F32),
            jax.ShapeDtypeStruct((leaves,), jnp.int32),
        ),
        in_specs=[pl.BlockSpec(memory_space=pltpu.SMEM), vmem, vmem, vmem],
        out_specs=(vmem, pl.BlockSpec(memory_space=pltpu.SMEM)),
        scratch_shapes=[pltpu.SMEM((devices,), jnp.int32), pltpu.VMEM((leaves, 4), F32)],
        compiler_params=pltpu.CompilerParams(vmem_limit_bytes=14 << 20),
        name="pack",
    )(owner, coords, charge, center)


def leaf_kernel(which, stacked, m2l, leaf, dens):
    leaves, width = m2l.shape
    dens[...] = jnp.zeros_like(dens)

    def place(j, carry):
        row = m2l[pl.ds(j, 1), :] + stacked[pl.ds(which[j], 1), :]
        leaf[pl.ds(j, 1), :] = row
        dens[pl.ds(j, 1), 0:width] = row
        return carry

    lax.fori_loop(0, leaves, place, 0, unroll=8)


def leaf_rows(which, stacked, m2l, padded):
    vmem = pl.BlockSpec(memory_space=pltpu.VMEM)
    smem = pl.BlockSpec(memory_space=pltpu.SMEM)
    return pl.pallas_call(
        leaf_kernel,
        out_shape=(
            jax.ShapeDtypeStruct(m2l.shape, F32),
            jax.ShapeDtypeStruct((m2l.shape[0], padded), F32),
        ),
        in_specs=[smem, vmem, vmem],
        out_specs=(vmem, vmem),
        compiler_params=pltpu.CompilerParams(vmem_limit_bytes=14 << 20),
        cost_estimate=pl.CostEstimate(flops=1 << 18, bytes_accessed=8 << 20, transcendentals=0),
        name="leaf_rows",
    )(which, stacked, m2l)


def split3(v):
    high = v.astype(BF16).astype(F32)
    rest = v - high
    middle = rest.astype(BF16).astype(F32)
    return high, middle, rest - middle


def target_features(x, y, z, extra):
    out = []
    for v in (x, y, z):
        h, m, l = split3(v)
        out += [h, h, h, m, m, l]
    return out + list(split3(x * x + y * y + z * z + extra))


def source_features(x, y, z):
    out = []
    for v in (x, y, z):
        h, m, l = split3(-2.0 * v)
        out += [h, m, l, h, m, h]
    return out, list(split3(x * x + y * y + z * z))


def near_kernel(group, unroll, near_list, src, off, out, table, charges, tfeat, sfeat):
    step = pl.program_id(0)
    senders, _, cap, _ = src.shape
    slots = senders * cap
    ones = jnp.ones((8, 128), F32)
    zeros = jnp.zeros((8, 128), F32)

    @pl.when(step == 0)
    def _():
        for f in range(18, 21):
            sfeat[8 * f : 8 * f + 8] = ones
        for f in range(24, FEATURES):
            sfeat[8 * f : 8 * f + 8] = zeros
        for u in range(unroll):
            for f in range(21, 24):
                tfeat[u, 8 * f : 8 * f + 8] = ones
            for f in range(24, FEATURES):
                tfeat[u, 8 * f : 8 * f + 8] = zeros

        def prepare(i, carry):
            cross, square = source_features(*(src[i, c] - 1.0 for c in range(3)))
            for f, v in list(enumerate(cross)) + list(enumerate(square, 21)):
                sfeat[8 * f : 8 * f + 8] = v
            for s in range(8):
                table[i * 8 + s] = sfeat[pl.ds(s, FEATURES, stride=8), :].astype(BF16)
            charges[pl.ds(i * 8, 8)] = src[i, 3] * (0.25 / math.pi)
            return carry

        lax.fori_loop(0, senders, prepare, 0)

    lane_part = lax.broadcasted_iota(jnp.int32, (128, 128), 1) // FEATURES

    def rows(i, carry):
        for u in range(unroll):
            local = i * unroll + u
            block = step * group + local
            info = src[block, 4]
            place = [
                (info[:, c : c + 1] - 1.0) + HALF * off[c, pl.ds(local * 8, 8), :] for c in range(3)
            ]
            for f, v in enumerate(target_features(*place, SOFT_SQ)):
                tfeat[u, 8 * f : 8 * f + 8] = v
            for s in range(8):
                feat = tfeat[u, pl.ds(s, FEATURES, stride=8), :]
                turned = jnp.concatenate([feat.astype(BF16)] * 4, axis=0).T
                left = jnp.concatenate(
                    [jnp.where(lane_part == k, turned, jnp.zeros_like(turned)) for k in range(4)],
                    axis=0,
                )
                at = [near_list[j * slots + block * 8 + s] for j in range(8)]
                right = jnp.concatenate(
                    [
                        jnp.concatenate([table[at[2 * k]], table[at[2 * k + 1]]], axis=1)
                        for k in range(4)
                    ],
                    axis=0,
                )
                dist_sq = jnp.dot(left, right, preferred_element_type=F32)
                total = None
                for k in range(4):
                    for h in range(2):
                        weight = charges[pl.ds(at[2 * k + h], 1), :]
                        part = dist_sq[128 * k : 128 * k + 128, 128 * h : 128 * h + 128]
                        term = lax.rsqrt(part) * weight
                        total = term if total is None else total + term
                out[pl.ds(local * 8 + s, 1), :] = jnp.sum(total.T, axis=0, keepdims=True)
            live = info[:, 3:4] > 0.5
            out[pl.ds(local * 8, 8), :] = jnp.where(live, out[pl.ds(local * 8, 8), :], 0.0)
        return carry

    lax.fori_loop(0, group // unroll, rows, 0)


def near_field(src, offsets, near_slots, group=16, unroll=4):
    senders, _, cap, _ = src.shape
    slots = senders * cap
    return pl.pallas_call(
        functools.partial(near_kernel, group, unroll),
        out_shape=jax.ShapeDtypeStruct((slots, 128), F32),
        grid_spec=pltpu.PrefetchScalarGridSpec(
            num_scalar_prefetch=1,
            grid=(senders // group,),
            in_specs=[
                pl.BlockSpec(src.shape, lambda g, n: (0, 0, 0, 0)),
                pl.BlockSpec((3, group * cap, 128), lambda g, n: (0, g, 0)),
            ],
            out_specs=pl.BlockSpec((group * cap, 128), lambda g, n: (g, 0)),
            scratch_shapes=[
                pltpu.VMEM((slots, FEATURES, 128), BF16),
                pltpu.VMEM((slots, 128), F32),
                pltpu.VMEM((unroll, FEATURES * 8, 128), F32),
                pltpu.VMEM((FEATURES * 8, 128), F32),
            ],
        ),
        compiler_params=pltpu.CompilerParams(vmem_limit_bytes=28 << 20),
        cost_estimate=pl.CostEstimate(
            flops=2 * slots * 512 * 128 * 256, bytes_accessed=8 << 20, transcendentals=slots << 17
        ),
        name="near_field",
    )(near_slots, src, offsets)


def surface_weights():
    grid = np.linspace(-1.0, 1.0, ORDER)
    points = np.stack(np.meshgrid(grid, grid, grid, indexing="ij"), 0).reshape(3, -1)
    on_surface = np.max(np.abs(points), axis=0) > 1.0 - 1e-09
    points = (points[:, on_surface] * RADIUS).astype(np.float32)
    fill = 320 - points.shape[1]
    points = np.concatenate([points, np.repeat(points[:, :1], fill, axis=1)], axis=1)

    def split(v):
        high = v.astype(ml_dtypes.bfloat16).astype(np.float32)
        rest = v - high
        middle = rest.astype(ml_dtypes.bfloat16).astype(np.float32)
        return high, middle, rest - middle

    rows = []
    for c in range(3):
        h, m, l = split(-2.0 * points[c])
        rows += [h, m, l, h, m, h]
    rows += [np.ones(320, np.float32)] * 3
    rows += list(split(np.sum(points * points, axis=0)))
    rows += [np.zeros(320, np.float32)] * (FEATURES - len(rows))
    rows = np.stack(rows)
    main = np.repeat(rows[:, :256], 8, axis=0)
    last = np.zeros((FEATURES, 8, 512), np.float32)
    for s in range(8):
        last[:, s, 64 * s : 64 * s + 64] = rows[:, 256:]
    last = last.reshape(FEATURES * 8, 512)
    return main.astype(ml_dtypes.bfloat16), last.astype(ml_dtypes.bfloat16)


def far_kernel(unroll, dest, off, dens, main, last, out, tfeat, shift):
    ones = jnp.ones((8, 128), F32)
    zeros = jnp.zeros((8, 128), F32)
    out[...] = jnp.zeros_like(out)
    for u in range(unroll):
        for f in range(21, 24):
            tfeat[u, 8 * f : 8 * f + 8] = ones
        for f in range(24, FEATURES):
            tfeat[u, 8 * f : 8 * f + 8] = zeros
    row_of_lane = lax.broadcasted_iota(jnp.int32, (128, 8 * FEATURES), 1) % 8
    low_half = lax.broadcasted_iota(jnp.int32, (1, 128), 1) < 64

    def rows(i, carry):
        for u in range(unroll):
            first = (i * unroll + u) * 8
            at = [dest[first + t] for t in range(8)]
            for t in range(8):
                for c in range(3):
                    shift[u, c, t : t + 1, :] = off[at[t] // 8, c, pl.ds(at[t] % 8, 1), :]
            for f, v in enumerate(target_features(*(shift[u, c] for c in range(3)), 0.0)):
                tfeat[u, 8 * f : 8 * f + 8] = v
            turned = tfeat[u].astype(BF16).T
            weights = [dens[pl.ds(first + t, 1), :] for t in range(8)]
            tail_sq = jnp.dot(turned, last[...], preferred_element_type=F32)
            for p in range(4):
                pair = jnp.where(
                    low_half,
                    weights[2 * p][:, 256:384],
                    pltpu.roll(weights[2 * p + 1][:, 256:384], 64, 1),
                )
                tail = lax.rsqrt(tail_sq[:, 128 * p : 128 * p + 128]) * pair
                for h in range(2):
                    t = 2 * p + h
                    left = jnp.where(row_of_lane == t, turned, jnp.zeros_like(turned))
                    dist_sq = jnp.dot(left, main[...], preferred_element_type=F32)
                    total = lax.rsqrt(dist_sq[:, :128]) * weights[t][:, :128]
                    total = total + lax.rsqrt(dist_sq[:, 128:]) * weights[t][:, 128:256]
                    total = total + jnp.where(low_half == (h == 0), tail, 0.0)
                    line = jnp.sum(total.T, axis=0, keepdims=True)
                    out[pl.ds(at[t], 1), :] = line * (0.25 / (math.pi * HALF))
        return carry

    lax.fori_loop(0, dens.shape[0] // (8 * unroll), rows, 0)


def far_field(dest, offsets, dens, unroll=4):
    devices, _, cap, points = offsets.shape
    main, last = surface_weights()
    vmem = pl.BlockSpec(memory_space=pltpu.VMEM)
    return pl.pallas_call(
        functools.partial(far_kernel, unroll),
        out_shape=jax.ShapeDtypeStruct((devices * cap, points), F32),
        in_specs=[pl.BlockSpec(memory_space=pltpu.SMEM)] + [vmem] * 4,
        out_specs=vmem,
        scratch_shapes=[
            pltpu.VMEM((unroll, FEATURES * 8, 128), F32),
            pltpu.VMEM((unroll, 3, 8, 128), F32),
        ],
        compiler_params=pltpu.CompilerParams(vmem_limit_bytes=14 << 20),
        cost_estimate=pl.CostEstimate(
            flops=2 * dens.shape[0] * 128 * 256 * 384,
            bytes_accessed=4 << 20,
            transcendentals=dens.shape[0] * 128 * 320,
        ),
        name="far_field",
    )(dest, offsets, dens, jnp.asarray(main), jnp.asarray(last))


def on_device(
    parent_local,
    parent_slot,
    child_octant,
    child_m2l,
    l2l_ops,
    leaf_center,
    src_coords,
    src_charge,
    obs_owner,
    obs_offset,
    near_slots,
):
    devices = lax.axis_size(AXES)
    leaf_dev, width = child_m2l.shape
    slots, _, points = obs_offset.shape
    cap = slots // devices
    me = lax.axis_index(AXES)
    mine = lax.dynamic_slice_in_dim(obs_owner, me * leaf_dev, leaf_dev)

    rim = from_behind(parent_local[parent_local.shape[0] - RIM :], AXES, 1)
    packed, dest = pack(mine, jnp.transpose(src_coords, (1, 0, 2)), src_charge, leaf_center, devices, cap)

    offsets = jnp.transpose(obs_offset, (1, 0, 2))
    outgoing = jnp.transpose(offsets.reshape(3, devices, cap, points), (1, 0, 2, 3))
    outgoing, rim = lax.optimization_barrier((outgoing, rim))
    at_leaves = lax.all_to_all(outgoing, AXES, 0, 0, tiled=True)

    parents = jnp.concatenate([rim, parent_local], axis=0)
    moved = jnp.einsum("pr,oqr->opq", parents, l2l_ops, precision=lax.Precision.HIGHEST)
    stacked = moved.reshape(l2l_ops.shape[0] * parents.shape[0], width)
    which = child_octant * parents.shape[0] + parent_slot
    leaf_local, dens = leaf_rows(which, stacked, child_m2l, 384)
    packed, dens = lax.optimization_barrier((packed, dens))
    received = lax.all_to_all(packed, AXES, 0, 0, tiled=True)
    far = far_field(dest, at_leaves, dens)
    received, far = lax.optimization_barrier((received, far))
    far = lax.all_to_all(far.reshape(devices, cap, points), AXES, 0, 0, tiled=True)

    near = near_field(received, offsets, jnp.transpose(near_slots).reshape(-1))
    return (leaf_local, near + far.reshape(slots, points))


def solution(mesh):
    placed = (
        P(AXES, None),
        P(AXES),
        P(AXES),
        P(AXES, None),
        P(),
        P(AXES, None),
        P(AXES, None, None),
        P(AXES, None),
        P(),
        P(AXES, None, None),
        P(AXES, None),
    )
    return jax.shard_map(
        on_device,
        mesh=mesh,
        in_specs=placed,
        out_specs=(P(AXES, None), P(AXES, None)),
        check_vma=False,
    )
```

```python
import functools
import math

import jax
import jax.numpy as jnp
import ml_dtypes
import numpy as np
from jax import lax
from jax.experimental import pallas as pl
from jax.experimental.pallas import tpu as pltpu
from jax.sharding import PartitionSpec as P

ORDER = 8
RIM = 16
RADIUS = 2.95
HALF = 0.5
SOFT_SQ = 0.0025
AXES = ("grp", "dom")
F32 = jnp.float32
BF16 = jnp.bfloat16
FEATURES = 32
MESH = pl.DeviceIdType.MESH


def from_behind(block, axis, distance):
    devices = range(lax.axis_size(axis))
    route = [(i - distance, i) for i in devices if i - distance in devices]
    return lax.ppermute(block, axis, route)


def pack_kernel(capacity, owner, coords, charge, center, out, dest, count, tail):
    devices = out.shape[0]
    leaves = charge.shape[0]
    out[...] = jnp.zeros_like(out)
    tail[:, 0:3] = center[...]
    tail[:, 3:4] = jnp.ones((leaves, 1), F32)

    def clear(i, carry):
        count[i] = 0
        return carry

    lax.fori_loop(0, devices, clear, 0, unroll=8)

    def place(j, carry):
        o = owner[j]
        rank = count[o]
        count[o] = rank + 1
        dest[j] = o * capacity + rank
        for c in range(3):
            out[o, c, pl.ds(rank, 1), :] = coords[c, pl.ds(j, 1), :]
        out[o, 3, pl.ds(rank, 1), :] = charge[pl.ds(j, 1), :]
        out[o, 4, pl.ds(rank, 1), 0:4] = tail[pl.ds(j, 1), :]
        return carry

    lax.fori_loop(0, leaves, place, 0, unroll=4)


def pack(owner, coords, charge, center, devices, capacity):
    leaves = charge.shape[0]
    vmem = pl.BlockSpec(memory_space=pltpu.VMEM)
    return pl.pallas_call(
        functools.partial(pack_kernel, capacity),
        out_shape=(
            jax.ShapeDtypeStruct((devices, 5, capacity, 128), F32),
            jax.ShapeDtypeStruct((leaves,), jnp.int32),
        ),
        in_specs=[pl.BlockSpec(memory_space=pltpu.SMEM), vmem, vmem, vmem],
        out_specs=(vmem, pl.BlockSpec(memory_space=pltpu.SMEM)),
        scratch_shapes=[pltpu.SMEM((devices,), jnp.int32), pltpu.VMEM((leaves, 4), F32)],
        compiler_params=pltpu.CompilerParams(vmem_limit_bytes=14 << 20),
        name="pack",
    )(owner, coords, charge, center)


def leaf_kernel(which, stacked, m2l, leaf, dens):
    leaves, width = m2l.shape
    dens[...] = jnp.zeros_like(dens)

    def place(j, carry):
        row = m2l[pl.ds(j, 1), :] + stacked[pl.ds(which[j], 1), :]
        leaf[pl.ds(j, 1), :] = row
        dens[pl.ds(j, 1), 0:width] = row
        return carry

    lax.fori_loop(0, leaves, place, 0, unroll=8)


def leaf_rows(which, stacked, m2l, padded):
    vmem = pl.BlockSpec(memory_space=pltpu.VMEM)
    smem = pl.BlockSpec(memory_space=pltpu.SMEM)
    return pl.pallas_call(
        leaf_kernel,
        out_shape=(
            jax.ShapeDtypeStruct(m2l.shape, F32),
            jax.ShapeDtypeStruct((m2l.shape[0], padded), F32),
        ),
        in_specs=[smem, vmem, vmem],
        out_specs=(vmem, vmem),
        compiler_params=pltpu.CompilerParams(vmem_limit_bytes=14 << 20),
        cost_estimate=pl.CostEstimate(flops=1 << 18, bytes_accessed=8 << 20, transcendentals=0),
        name="leaf_rows",
    )(which, stacked, m2l)


def split3(v):
    high = v.astype(BF16).astype(F32)
    rest = v - high
    middle = rest.astype(BF16).astype(F32)
    return high, middle, rest - middle


def target_features(x, y, z, extra):
    out = []
    for v in (x, y, z):
        h, m, l = split3(v)
        out += [h, h, h, m, m, l]
    return out + list(split3(x * x + y * y + z * z + extra))


def source_features(x, y, z):
    out = []
    for v in (x, y, z):
        h, m, l = split3(-2.0 * v)
        out += [h, m, l, h, m, h]
    return out, list(split3(x * x + y * y + z * z))


def peer_of(me, k, devices, inner):
    peer = lax.rem(me + k, devices)
    return peer, (peer // inner, lax.rem(peer, inner))


def near_kernel(
    unroll, inner, near_list, src, off, far, out, table, charges, tfeat, sfeat, arrived, sent, got
):
    senders, _, cap, _ = src.shape
    slots = senders * cap
    me = lax.axis_index("grp") * inner + lax.axis_index("dom")
    ones = jnp.ones((8, 128), F32)
    zeros = jnp.zeros((8, 128), F32)
    barrier = pltpu.get_barrier_semaphore()

    def greet(k, carry):
        _, device = peer_of(me, k, senders, inner)
        pl.semaphore_signal(barrier, inc=1, device_id=device, device_id_type=MESH)
        return carry

    lax.fori_loop(1, senders, greet, 0)

    for f in range(18, 21):
        sfeat[8 * f : 8 * f + 8] = ones
    for f in range(24, FEATURES):
        sfeat[8 * f : 8 * f + 8] = zeros
    for u in range(unroll):
        for f in range(21, 24):
            tfeat[u, 8 * f : 8 * f + 8] = ones
        for f in range(24, FEATURES):
            tfeat[u, 8 * f : 8 * f + 8] = zeros

    def prepare(i, carry):
        cross, square = source_features(*(src[i, c] - 1.0 for c in range(3)))
        for f, v in list(enumerate(cross)) + list(enumerate(square, 21)):
            sfeat[8 * f : 8 * f + 8] = v
        for s in range(8):
            table[i * 8 + s] = sfeat[pl.ds(s, FEATURES, stride=8), :].astype(BF16)
        charges[pl.ds(i * 8, 8)] = src[i, 3] * (0.25 / math.pi)
        return carry

    lax.fori_loop(0, senders, prepare, 0)
    pl.semaphore_wait(barrier, senders - 1)

    def send(k):
        peer, device = peer_of(me, k, senders, inner)
        pltpu.make_async_remote_copy(
            src_ref=far.at[peer],
            dst_ref=arrived.at[me],
            send_sem=sent,
            recv_sem=got,
            device_id=device,
            device_id_type=MESH,
        ).start()

    rounds = senders // unroll
    inline = (senders - 1) // rounds
    early = senders - rounds * inline

    def send_early(k, carry):
        send(k)
        return carry

    lax.fori_loop(1, early, send_early, 0)
    lane_part = lax.broadcasted_iota(jnp.int32, (128, 128), 1) // FEATURES

    def rows(i, carry):
        for u in range(unroll):
            if u < inline:
                send(early + i * inline + u)
            block = i * unroll + u
            info = src[block, 4]
            place = [
                (info[:, c : c + 1] - 1.0) + HALF * off[c, pl.ds(block * 8, 8), :] for c in range(3)
            ]
            for f, v in enumerate(target_features(*place, SOFT_SQ)):
                tfeat[u, 8 * f : 8 * f + 8] = v
            for s in range(8):
                feat = tfeat[u, pl.ds(s, FEATURES, stride=8), :]
                turned = jnp.concatenate([feat.astype(BF16)] * 4, axis=0).T
                left = jnp.concatenate(
                    [jnp.where(lane_part == k, turned, jnp.zeros_like(turned)) for k in range(4)],
                    axis=0,
                )
                at = [near_list[j * slots + block * 8 + s] for j in range(8)]
                right = jnp.concatenate(
                    [
                        jnp.concatenate([table[at[2 * k]], table[at[2 * k + 1]]], axis=1)
                        for k in range(4)
                    ],
                    axis=0,
                )
                dist_sq = jnp.dot(left, right, preferred_element_type=F32)
                total = None
                for k in range(4):
                    for h in range(2):
                        weight = charges[pl.ds(at[2 * k + h], 1), :]
                        part = dist_sq[128 * k : 128 * k + 128, 128 * h : 128 * h + 128]
                        term = lax.rsqrt(part) * weight
                        total = term if total is None else total + term
                out[pl.ds(block * 8 + s, 1), :] = jnp.sum(total.T, axis=0, keepdims=True)
            live = info[:, 3:4] > 0.5
            out[pl.ds(block * 8, 8), :] = jnp.where(live, out[pl.ds(block * 8, 8), :], 0.0)
        return carry

    lax.fori_loop(0, rounds, rows, 0)

    everything = pltpu.make_async_remote_copy(
        src_ref=far.at[pl.ds(0, senders - 1)],
        dst_ref=arrived.at[pl.ds(0, senders - 1)],
        send_sem=sent,
        recv_sem=got,
        device_id=peer_of(me, 1, senders, inner)[1],
        device_id_type=MESH,
    )
    everything.wait_send()
    everything.wait_recv()
    arrived[me] = far[me]

    def add(i, carry):
        out[pl.ds(i * 8, 8), :] += arrived[i]
        return carry

    lax.fori_loop(0, senders, add, 0, unroll=8)


def near_field(src, offsets, near_list, far, inner, unroll=8):
    senders, _, cap, _ = src.shape
    slots = senders * cap
    vmem = pl.BlockSpec(memory_space=pltpu.VMEM)
    return pl.pallas_call(
        functools.partial(near_kernel, unroll, inner),
        out_shape=jax.ShapeDtypeStruct((slots, 128), F32),
        in_specs=[pl.BlockSpec(memory_space=pltpu.SMEM), vmem, vmem, vmem],
        out_specs=vmem,
        scratch_shapes=[
            pltpu.VMEM((slots, FEATURES, 128), BF16),
            pltpu.VMEM((slots, 128), F32),
            pltpu.VMEM((unroll, FEATURES * 8, 128), F32),
            pltpu.VMEM((FEATURES * 8, 128), F32),
            pltpu.VMEM((senders, cap, 128), F32),
            pltpu.SemaphoreType.DMA,
            pltpu.SemaphoreType.DMA,
        ],
        compiler_params=pltpu.CompilerParams(
            vmem_limit_bytes=28 << 20, collective_id=0, has_side_effects=True
        ),
        cost_estimate=pl.CostEstimate(
            flops=2 * slots * 512 * 128 * 256, bytes_accessed=8 << 20, transcendentals=slots << 17
        ),
        name="near_field",
    )(near_list, src, offsets, far)


def surface_weights():
    grid = np.linspace(-1.0, 1.0, ORDER)
    points = np.stack(np.meshgrid(grid, grid, grid, indexing="ij"), 0).reshape(3, -1)
    on_surface = np.max(np.abs(points), axis=0) > 1.0 - 1e-09
    points = (points[:, on_surface] * RADIUS).astype(np.float32)
    fill = 320 - points.shape[1]
    points = np.concatenate([points, np.repeat(points[:, :1], fill, axis=1)], axis=1)

    def split(v):
        high = v.astype(ml_dtypes.bfloat16).astype(np.float32)
        rest = v - high
        middle = rest.astype(ml_dtypes.bfloat16).astype(np.float32)
        return high, middle, rest - middle

    rows = []
    for c in range(3):
        h, m, l = split(-2.0 * points[c])
        rows += [h, m, l, h, m, h]
    rows += [np.ones(320, np.float32)] * 3
    rows += list(split(np.sum(points * points, axis=0)))
    rows += [np.zeros(320, np.float32)] * (FEATURES - len(rows))
    rows = np.stack(rows)
    main = np.repeat(rows[:, :256], 8, axis=0)
    last = np.zeros((FEATURES, 8, 512), np.float32)
    for s in range(8):
        last[:, s, 64 * s : 64 * s + 64] = rows[:, 256:]
    last = last.reshape(FEATURES * 8, 512)
    return main.astype(ml_dtypes.bfloat16), last.astype(ml_dtypes.bfloat16)


def far_kernel(unroll, dest, off, dens, main, last, out, tfeat, shift):
    ones = jnp.ones((8, 128), F32)
    zeros = jnp.zeros((8, 128), F32)
    out[...] = jnp.zeros_like(out)
    for u in range(unroll):
        for f in range(21, 24):
            tfeat[u, 8 * f : 8 * f + 8] = ones
        for f in range(24, FEATURES):
            tfeat[u, 8 * f : 8 * f + 8] = zeros
    row_of_lane = lax.broadcasted_iota(jnp.int32, (128, 8 * FEATURES), 1) % 8
    low_half = lax.broadcasted_iota(jnp.int32, (1, 128), 1) < 64

    def rows(i, carry):
        for u in range(unroll):
            first = (i * unroll + u) * 8
            at = [dest[first + t] for t in range(8)]
            for t in range(8):
                for c in range(3):
                    shift[u, c, t : t + 1, :] = off[at[t] // 8, c, pl.ds(at[t] % 8, 1), :]
            for f, v in enumerate(target_features(*(shift[u, c] for c in range(3)), 0.0)):
                tfeat[u, 8 * f : 8 * f + 8] = v
            turned = tfeat[u].astype(BF16).T
            weights = [dens[pl.ds(first + t, 1), :] for t in range(8)]
            tail_sq = jnp.dot(turned, last[...], preferred_element_type=F32)
            for p in range(4):
                pair = jnp.where(
                    low_half,
                    weights[2 * p][:, 256:384],
                    pltpu.roll(weights[2 * p + 1][:, 256:384], 64, 1),
                )
                tail = lax.rsqrt(tail_sq[:, 128 * p : 128 * p + 128]) * pair
                for h in range(2):
                    t = 2 * p + h
                    left = jnp.where(row_of_lane == t, turned, jnp.zeros_like(turned))
                    dist_sq = jnp.dot(left, main[...], preferred_element_type=F32)
                    total = lax.rsqrt(dist_sq[:, :128]) * weights[t][:, :128]
                    total = total + lax.rsqrt(dist_sq[:, 128:]) * weights[t][:, 128:256]
                    total = total + jnp.where(low_half == (h == 0), tail, 0.0)
                    line = jnp.sum(total.T, axis=0, keepdims=True)
                    out[pl.ds(at[t], 1), :] = line * (0.25 / (math.pi * HALF))
        return carry

    lax.fori_loop(0, dens.shape[0] // (8 * unroll), rows, 0)


def far_field(dest, offsets, dens, unroll=4):
    devices, _, cap, points = offsets.shape
    main, last = surface_weights()
    vmem = pl.BlockSpec(memory_space=pltpu.VMEM)
    return pl.pallas_call(
        functools.partial(far_kernel, unroll),
        out_shape=jax.ShapeDtypeStruct((devices * cap, points), F32),
        in_specs=[pl.BlockSpec(memory_space=pltpu.SMEM)] + [vmem] * 4,
        out_specs=vmem,
        scratch_shapes=[
            pltpu.VMEM((unroll, FEATURES * 8, 128), F32),
            pltpu.VMEM((unroll, 3, 8, 128), F32),
        ],
        compiler_params=pltpu.CompilerParams(vmem_limit_bytes=14 << 20),
        cost_estimate=pl.CostEstimate(
            flops=2 * dens.shape[0] * 128 * 256 * 384,
            bytes_accessed=4 << 20,
            transcendentals=dens.shape[0] * 128 * 320,
        ),
        name="far_field",
    )(dest, offsets, dens, jnp.asarray(main), jnp.asarray(last))


def on_device(
    parent_local,
    parent_slot,
    child_octant,
    child_m2l,
    l2l_ops,
    leaf_center,
    src_coords,
    src_charge,
    obs_owner,
    obs_offset,
    near_slots,
):
    devices = lax.axis_size(AXES)
    leaf_dev, width = child_m2l.shape
    slots, _, points = obs_offset.shape
    cap = slots // devices
    me = lax.axis_index(AXES)
    mine = lax.dynamic_slice_in_dim(obs_owner, me * leaf_dev, leaf_dev)

    rim = from_behind(parent_local[parent_local.shape[0] - RIM :], AXES, 1)
    packed, dest = pack(mine, jnp.transpose(src_coords, (1, 0, 2)), src_charge, leaf_center, devices, cap)

    offsets = jnp.transpose(obs_offset, (1, 0, 2))
    outgoing = jnp.transpose(offsets.reshape(3, devices, cap, points), (1, 0, 2, 3))
    outgoing, rim = lax.optimization_barrier((outgoing, rim))
    at_leaves = lax.all_to_all(outgoing, AXES, 0, 0, tiled=True)

    parents = jnp.concatenate([rim, parent_local], axis=0)
    moved = jnp.einsum("pr,oqr->opq", parents, l2l_ops, precision=lax.Precision.HIGHEST)
    stacked = moved.reshape(l2l_ops.shape[0] * parents.shape[0], width)
    which = child_octant * parents.shape[0] + parent_slot
    leaf_local, dens = leaf_rows(which, stacked, child_m2l, 384)
    packed, dens = lax.optimization_barrier((packed, dens))
    received = lax.all_to_all(packed, AXES, 0, 0, tiled=True)
    far = far_field(dest, at_leaves, dens)
    far = far.reshape(devices, cap, points)
    near_list = jnp.transpose(near_slots).reshape(-1)
    potential = near_field(received, offsets, near_list, far, lax.axis_size("dom"))
    return (leaf_local, potential)


def solution(mesh):
    placed = (
        P(AXES, None),
        P(AXES),
        P(AXES),
        P(AXES, None),
        P(),
        P(AXES, None),
        P(AXES, None, None),
        P(AXES, None),
        P(),
        P(AXES, None, None),
        P(AXES, None),
    )
    return jax.shard_map(
        on_device,
        mesh=mesh,
        in_specs=placed,
        out_specs=(P(AXES, None), P(AXES, None)),
        check_vma=False,
    )
```

```python
import functools
import math

import jax
import jax.numpy as jnp
import ml_dtypes
import numpy as np
from jax import lax
from jax.experimental import pallas as pl
from jax.experimental.pallas import tpu as pltpu
from jax.sharding import PartitionSpec as P

ORDER = 8
RIM = 16
RADIUS = 2.95
HALF = 0.5
SOFT_SQ = 0.0025
AXES = ("grp", "dom")
F32 = jnp.float32
BF16 = jnp.bfloat16
FEATURES = 32
MESH = pl.DeviceIdType.MESH


def from_behind(block, axis, distance):
    devices = range(lax.axis_size(axis))
    route = [(i - distance, i) for i in devices if i - distance in devices]
    return lax.ppermute(block, axis, route)


def pack_kernel(capacity, owner, coords, charge, center, out, dest, count, tail):
    devices = out.shape[0]
    leaves = charge.shape[0]
    out[...] = jnp.zeros_like(out)
    tail[:, 0:3] = center[...]
    tail[:, 3:4] = jnp.ones((leaves, 1), F32)

    def clear(i, carry):
        count[i] = 0
        return carry

    lax.fori_loop(0, devices, clear, 0, unroll=8)

    def place(j, carry):
        o = owner[j]
        rank = count[o]
        count[o] = rank + 1
        dest[j] = o * capacity + rank
        for c in range(3):
            out[o, c, pl.ds(rank, 1), :] = coords[c, pl.ds(j, 1), :]
        out[o, 3, pl.ds(rank, 1), :] = charge[pl.ds(j, 1), :]
        out[o, 4, pl.ds(rank, 1), 0:4] = tail[pl.ds(j, 1), :]
        return carry

    lax.fori_loop(0, leaves, place, 0, unroll=4)


def pack(owner, coords, charge, center, devices, capacity):
    leaves = charge.shape[0]
    vmem = pl.BlockSpec(memory_space=pltpu.VMEM)
    return pl.pallas_call(
        functools.partial(pack_kernel, capacity),
        out_shape=(
            jax.ShapeDtypeStruct((devices, 5, capacity, 128), F32),
            jax.ShapeDtypeStruct((leaves,), jnp.int32),
        ),
        in_specs=[pl.BlockSpec(memory_space=pltpu.SMEM), vmem, vmem, vmem],
        out_specs=(vmem, pl.BlockSpec(memory_space=pltpu.SMEM)),
        scratch_shapes=[pltpu.SMEM((devices,), jnp.int32), pltpu.VMEM((leaves, 4), F32)],
        compiler_params=pltpu.CompilerParams(vmem_limit_bytes=14 << 20),
        name="pack",
    )(owner, coords, charge, center)


def leaf_kernel(which, stacked, m2l, leaf, dens):
    leaves, width = m2l.shape
    dens[...] = jnp.zeros_like(dens)

    def place(j, carry):
        row = m2l[pl.ds(j, 1), :] + stacked[pl.ds(which[j], 1), :]
        leaf[pl.ds(j, 1), :] = row
        dens[pl.ds(j, 1), 0:width] = row
        return carry

    lax.fori_loop(0, leaves, place, 0, unroll=8)


def leaf_rows(which, stacked, m2l, padded):
    vmem = pl.BlockSpec(memory_space=pltpu.VMEM)
    smem = pl.BlockSpec(memory_space=pltpu.SMEM)
    return pl.pallas_call(
        leaf_kernel,
        out_shape=(
            jax.ShapeDtypeStruct(m2l.shape, F32),
            jax.ShapeDtypeStruct((m2l.shape[0], padded), F32),
        ),
        in_specs=[smem, vmem, vmem],
        out_specs=(vmem, vmem),
        compiler_params=pltpu.CompilerParams(vmem_limit_bytes=14 << 20),
        cost_estimate=pl.CostEstimate(flops=1 << 18, bytes_accessed=8 << 20, transcendentals=0),
        name="leaf_rows",
    )(which, stacked, m2l)


def split3(v):
    high = v.astype(BF16).astype(F32)
    rest = v - high
    middle = rest.astype(BF16).astype(F32)
    return high, middle, rest - middle


def target_features(x, y, z, extra):
    out = []
    for v in (x, y, z):
        h, m, l = split3(v)
        out += [h, h, h, m, m, l]
    return out + list(split3(x * x + y * y + z * z + extra))


def source_features(x, y, z):
    out = []
    for v in (x, y, z):
        h, m, l = split3(-2.0 * v)
        out += [h, m, l, h, m, h]
    return out, list(split3(x * x + y * y + z * z))


def peer_of(me, k, devices, inner):
    peer = lax.rem(me + k, devices)
    return peer, (peer // inner, lax.rem(peer, inner))


def near_kernel(
    unroll, inner, near_list, src, off, far, out, table, charges, tfeat, sfeat, arrived, sent, got
):
    senders, _, cap, _ = src.shape
    slots = senders * cap
    me = lax.axis_index("grp") * inner + lax.axis_index("dom")
    ones = jnp.ones((8, 128), F32)
    zeros = jnp.zeros((8, 128), F32)
    barrier = pltpu.get_barrier_semaphore()

    def greet(k, carry):
        _, device = peer_of(me, k, senders, inner)
        pl.semaphore_signal(barrier, inc=1, device_id=device, device_id_type=MESH)
        return carry

    lax.fori_loop(1, senders, greet, 0)

    for f in range(18, 21):
        sfeat[8 * f : 8 * f + 8] = ones
    for f in range(24, FEATURES):
        sfeat[8 * f : 8 * f + 8] = zeros
    for u in range(unroll):
        for f in range(21, 24):
            tfeat[u, 8 * f : 8 * f + 8] = ones
        for f in range(24, FEATURES):
            tfeat[u, 8 * f : 8 * f + 8] = zeros

    def prepare(i, carry):
        cross, square = source_features(*(src[i, c] - 1.0 for c in range(3)))
        for f, v in list(enumerate(cross)) + list(enumerate(square, 21)):
            sfeat[8 * f : 8 * f + 8] = v
        for s in range(8):
            table[i * 8 + s] = sfeat[pl.ds(s, FEATURES, stride=8), :].astype(BF16)
        charges[pl.ds(i * 8, 8)] = src[i, 3] * (0.25 / math.pi)
        return carry

    lax.fori_loop(0, senders, prepare, 0)
    pl.semaphore_wait(barrier, senders - 1)

    def send(k):
        peer, device = peer_of(me, k, senders, inner)
        pltpu.make_async_remote_copy(
            src_ref=far.at[peer],
            dst_ref=arrived.at[me],
            send_sem=sent,
            recv_sem=got,
            device_id=device,
            device_id_type=MESH,
        ).start()

    def send_all(k, carry):
        send(k)
        return carry

    lax.fori_loop(1, senders, send_all, 0)
    lane_part = lax.broadcasted_iota(jnp.int32, (128, 128), 1) // FEATURES

    def rows(i, carry):
        for u in range(unroll):
            block = i * unroll + u
            info = src[block, 4]
            place = [
                (info[:, c : c + 1] - 1.0) + HALF * off[c, pl.ds(block * 8, 8), :] for c in range(3)
            ]
            for f, v in enumerate(target_features(*place, SOFT_SQ)):
                tfeat[u, 8 * f : 8 * f + 8] = v
            for s in range(8):
                feat = tfeat[u, pl.ds(s, FEATURES, stride=8), :]
                turned = jnp.concatenate([feat.astype(BF16)] * 4, axis=0).T
                left = jnp.concatenate(
                    [jnp.where(lane_part == k, turned, jnp.zeros_like(turned)) for k in range(4)],
                    axis=0,
                )
                at = [near_list[j * slots + block * 8 + s] for j in range(8)]
                right = jnp.concatenate(
                    [
                        jnp.concatenate([table[at[2 * k]], table[at[2 * k + 1]]], axis=1)
                        for k in range(4)
                    ],
                    axis=0,
                )
                dist_sq = jnp.dot(left, right, preferred_element_type=F32)
                total = None
                for k in range(4):
                    for h in range(2):
                        weight = charges[pl.ds(at[2 * k + h], 1), :]
                        part = dist_sq[128 * k : 128 * k + 128, 128 * h : 128 * h + 128]
                        term = lax.rsqrt(part) * weight
                        total = term if total is None else total + term
                out[pl.ds(block * 8 + s, 1), :] = jnp.sum(total.T, axis=0, keepdims=True)
            live = info[:, 3:4] > 0.5
            out[pl.ds(block * 8, 8), :] = jnp.where(live, out[pl.ds(block * 8, 8), :], 0.0)
        return carry

    lax.fori_loop(0, senders // unroll, rows, 0)

    everything = pltpu.make_async_remote_copy(
        src_ref=far.at[pl.ds(0, senders - 1)],
        dst_ref=arrived.at[pl.ds(0, senders - 1)],
        send_sem=sent,
        recv_sem=got,
        device_id=peer_of(me, 1, senders, inner)[1],
        device_id_type=MESH,
    )
    everything.wait_send()
    everything.wait_recv()
    arrived[me] = far[me]

    def add(i, carry):
        out[pl.ds(i * 8, 8), :] += arrived[i]
        return carry

    lax.fori_loop(0, senders, add, 0, unroll=8)


def near_field(src, offsets, near_list, far, inner, unroll=8):
    senders, _, cap, _ = src.shape
    slots = senders * cap
    vmem = pl.BlockSpec(memory_space=pltpu.VMEM)
    return pl.pallas_call(
        functools.partial(near_kernel, unroll, inner),
        out_shape=jax.ShapeDtypeStruct((slots, 128), F32),
        in_specs=[pl.BlockSpec(memory_space=pltpu.SMEM), vmem, vmem, vmem],
        out_specs=vmem,
        scratch_shapes=[
            pltpu.VMEM((slots, FEATURES, 128), BF16),
            pltpu.VMEM((slots, 128), F32),
            pltpu.VMEM((unroll, FEATURES * 8, 128), F32),
            pltpu.VMEM((FEATURES * 8, 128), F32),
            pltpu.VMEM((senders, cap, 128), F32),
            pltpu.SemaphoreType.DMA,
            pltpu.SemaphoreType.DMA,
        ],
        compiler_params=pltpu.CompilerParams(
            vmem_limit_bytes=28 << 20, collective_id=0, has_side_effects=True
        ),
        cost_estimate=pl.CostEstimate(
            flops=2 * slots * 512 * 128 * 256, bytes_accessed=8 << 20, transcendentals=slots << 17
        ),
        name="near_field",
    )(near_list, src, offsets, far)


def surface_weights():
    grid = np.linspace(-1.0, 1.0, ORDER)
    points = np.stack(np.meshgrid(grid, grid, grid, indexing="ij"), 0).reshape(3, -1)
    on_surface = np.max(np.abs(points), axis=0) > 1.0 - 1e-09
    points = (points[:, on_surface] * RADIUS).astype(np.float32)
    fill = 320 - points.shape[1]
    points = np.concatenate([points, np.repeat(points[:, :1], fill, axis=1)], axis=1)

    def split(v):
        high = v.astype(ml_dtypes.bfloat16).astype(np.float32)
        rest = v - high
        middle = rest.astype(ml_dtypes.bfloat16).astype(np.float32)
        return high, middle, rest - middle

    rows = []
    for c in range(3):
        h, m, l = split(-2.0 * points[c])
        rows += [h, m, l, h, m, h]
    rows += [np.ones(320, np.float32)] * 3
    rows += list(split(np.sum(points * points, axis=0)))
    rows += [np.zeros(320, np.float32)] * (FEATURES - len(rows))
    rows = np.stack(rows)
    main = np.repeat(rows[:, :256], 8, axis=0)
    last = np.zeros((FEATURES, 8, 512), np.float32)
    for s in range(8):
        last[:, s, 64 * s : 64 * s + 64] = rows[:, 256:]
    last = last.reshape(FEATURES * 8, 512)
    return main.astype(ml_dtypes.bfloat16), last.astype(ml_dtypes.bfloat16)


def far_kernel(unroll, dest, off, dens, main, last, out, tfeat, shift):
    ones = jnp.ones((8, 128), F32)
    zeros = jnp.zeros((8, 128), F32)
    out[...] = jnp.zeros_like(out)
    for u in range(unroll):
        for f in range(21, 24):
            tfeat[u, 8 * f : 8 * f + 8] = ones
        for f in range(24, FEATURES):
            tfeat[u, 8 * f : 8 * f + 8] = zeros
    row_of_lane = lax.broadcasted_iota(jnp.int32, (128, 8 * FEATURES), 1) % 8
    low_half = lax.broadcasted_iota(jnp.int32, (1, 128), 1) < 64

    def rows(i, carry):
        for u in range(unroll):
            first = (i * unroll + u) * 8
            at = [dest[first + t] for t in range(8)]
            for t in range(8):
                for c in range(3):
                    shift[u, c, t : t + 1, :] = off[at[t] // 8, c, pl.ds(at[t] % 8, 1), :]
            for f, v in enumerate(target_features(*(shift[u, c] for c in range(3)), 0.0)):
                tfeat[u, 8 * f : 8 * f + 8] = v
            turned = tfeat[u].astype(BF16).T
            weights = [dens[pl.ds(first + t, 1), :] for t in range(8)]
            tail_sq = jnp.dot(turned, last[...], preferred_element_type=F32)
            for p in range(4):
                pair = jnp.where(
                    low_half,
                    weights[2 * p][:, 256:384],
                    pltpu.roll(weights[2 * p + 1][:, 256:384], 64, 1),
                )
                tail = lax.rsqrt(tail_sq[:, 128 * p : 128 * p + 128]) * pair
                for h in range(2):
                    t = 2 * p + h
                    left = jnp.where(row_of_lane == t, turned, jnp.zeros_like(turned))
                    dist_sq = jnp.dot(left, main[...], preferred_element_type=F32)
                    total = lax.rsqrt(dist_sq[:, :128]) * weights[t][:, :128]
                    total = total + lax.rsqrt(dist_sq[:, 128:]) * weights[t][:, 128:256]
                    total = total + jnp.where(low_half == (h == 0), tail, 0.0)
                    line = jnp.sum(total.T, axis=0, keepdims=True)
                    out[pl.ds(at[t], 1), :] = line * (0.25 / (math.pi * HALF))
        return carry

    lax.fori_loop(0, dens.shape[0] // (8 * unroll), rows, 0)


def far_field(dest, offsets, dens, unroll=4):
    devices, _, cap, points = offsets.shape
    main, last = surface_weights()
    vmem = pl.BlockSpec(memory_space=pltpu.VMEM)
    return pl.pallas_call(
        functools.partial(far_kernel, unroll),
        out_shape=jax.ShapeDtypeStruct((devices * cap, points), F32),
        in_specs=[pl.BlockSpec(memory_space=pltpu.SMEM)] + [vmem] * 4,
        out_specs=vmem,
        scratch_shapes=[
            pltpu.VMEM((unroll, FEATURES * 8, 128), F32),
            pltpu.VMEM((unroll, 3, 8, 128), F32),
        ],
        compiler_params=pltpu.CompilerParams(vmem_limit_bytes=14 << 20),
        cost_estimate=pl.CostEstimate(
            flops=2 * dens.shape[0] * 128 * 256 * 384,
            bytes_accessed=4 << 20,
            transcendentals=dens.shape[0] * 128 * 320,
        ),
        name="far_field",
    )(dest, offsets, dens, jnp.asarray(main), jnp.asarray(last))


def on_device(
    parent_local,
    parent_slot,
    child_octant,
    child_m2l,
    l2l_ops,
    leaf_center,
    src_coords,
    src_charge,
    obs_owner,
    obs_offset,
    near_slots,
):
    devices = lax.axis_size(AXES)
    leaf_dev, width = child_m2l.shape
    slots, _, points = obs_offset.shape
    cap = slots // devices
    me = lax.axis_index(AXES)
    mine = lax.dynamic_slice_in_dim(obs_owner, me * leaf_dev, leaf_dev)

    rim = from_behind(parent_local[parent_local.shape[0] - RIM :], AXES, 1)
    packed, dest = pack(mine, jnp.transpose(src_coords, (1, 0, 2)), src_charge, leaf_center, devices, cap)

    offsets = jnp.transpose(obs_offset, (1, 0, 2))
    outgoing = jnp.transpose(offsets.reshape(3, devices, cap, points), (1, 0, 2, 3))
    outgoing, rim = lax.optimization_barrier((outgoing, rim))
    at_leaves = lax.all_to_all(outgoing, AXES, 0, 0, tiled=True)

    parents = jnp.concatenate([rim, parent_local], axis=0)
    moved = jnp.einsum("pr,oqr->opq", parents, l2l_ops, precision=lax.Precision.HIGHEST)
    stacked = moved.reshape(l2l_ops.shape[0] * parents.shape[0], width)
    which = child_octant * parents.shape[0] + parent_slot
    leaf_local, dens = leaf_rows(which, stacked, child_m2l, 384)
    packed, dens = lax.optimization_barrier((packed, dens))
    received = lax.all_to_all(packed, AXES, 0, 0, tiled=True)
    far = far_field(dest, at_leaves, dens)
    far = far.reshape(devices, cap, points)
    near_list = jnp.transpose(near_slots).reshape(-1)
    potential = near_field(received, offsets, near_list, far, lax.axis_size("dom"))
    return (leaf_local, potential)


def solution(mesh):
    placed = (
        P(AXES, None),
        P(AXES),
        P(AXES),
        P(AXES, None),
        P(),
        P(AXES, None),
        P(AXES, None, None),
        P(AXES, None),
        P(),
        P(AXES, None, None),
        P(AXES, None),
    )
    return jax.shard_map(
        on_device,
        mesh=mesh,
        in_specs=placed,
        out_specs=(P(AXES, None), P(AXES, None)),
        check_vma=False,
    )
```

```python
import functools
import math

import jax
import jax.numpy as jnp
import ml_dtypes
import numpy as np
from jax import lax
from jax.experimental import pallas as pl
from jax.experimental.pallas import tpu as pltpu
from jax.sharding import PartitionSpec as P

ORDER = 8
RIM = 16
RADIUS = 2.95
HALF = 0.5
SOFT_SQ = 0.0025
AXES = ("grp", "dom")
F32 = jnp.float32
BF16 = jnp.bfloat16
FEATURES = 32
MESH = pl.DeviceIdType.MESH


def from_behind(block, axis, distance):
    devices = range(lax.axis_size(axis))
    route = [(i - distance, i) for i in devices if i - distance in devices]
    return lax.ppermute(block, axis, route)


def pack_kernel(capacity, owner, coords, charge, center, out, dest, slot_leaf, count, tail):
    devices = out.shape[0]
    leaves = charge.shape[0]
    out[...] = jnp.zeros_like(out)
    tail[:, 0:3] = center[...]
    tail[:, 3:4] = jnp.ones((leaves, 1), F32)

    def clear(i, carry):
        count[i] = 0
        for k in range(capacity):
            slot_leaf[i * capacity + k] = leaves
        return carry

    lax.fori_loop(0, devices, clear, 0, unroll=8)

    def place(j, carry):
        o = owner[j]
        rank = count[o]
        count[o] = rank + 1
        dest[j] = o * capacity + rank
        slot_leaf[o * capacity + rank] = j
        for c in range(3):
            out[o, c, pl.ds(rank, 1), :] = coords[c, pl.ds(j, 1), :]
        out[o, 3, pl.ds(rank, 1), :] = charge[pl.ds(j, 1), :]
        out[o, 4, pl.ds(rank, 1), 0:4] = tail[pl.ds(j, 1), :]
        return carry

    lax.fori_loop(0, leaves, place, 0, unroll=4)


def pack(owner, coords, charge, center, devices, capacity):
    leaves = charge.shape[0]
    vmem = pl.BlockSpec(memory_space=pltpu.VMEM)
    smem = pl.BlockSpec(memory_space=pltpu.SMEM)
    return pl.pallas_call(
        functools.partial(pack_kernel, capacity),
        out_shape=(
            jax.ShapeDtypeStruct((devices, 5, capacity, 128), F32),
            jax.ShapeDtypeStruct((leaves,), jnp.int32),
            jax.ShapeDtypeStruct((devices * capacity,), jnp.int32),
        ),
        in_specs=[smem, vmem, vmem, vmem],
        out_specs=(vmem, smem, smem),
        scratch_shapes=[pltpu.SMEM((devices,), jnp.int32), pltpu.VMEM((leaves, 4), F32)],
        compiler_params=pltpu.CompilerParams(vmem_limit_bytes=14 << 20),
        name="pack",
    )(owner, coords, charge, center)


def split3(v):
    high = v.astype(BF16).astype(F32)
    rest = v - high
    middle = rest.astype(BF16).astype(F32)
    return high, middle, rest - middle


def target_features(x, y, z, extra):
    out = []
    for v in (x, y, z):
        h, m, l = split3(v)
        out += [h, h, h, m, m, l]
    return out + list(split3(x * x + y * y + z * z + extra))


def source_features(x, y, z):
    out = []
    for v in (x, y, z):
        h, m, l = split3(-2.0 * v)
        out += [h, m, l, h, m, h]
    return out, list(split3(x * x + y * y + z * z))


def peer_of(me, k, devices, inner):
    peer = lax.rem(me + k, devices)
    return peer, (peer // inner, lax.rem(peer, inner))


def near_kernel(
    unroll, inner, near_list, src, off, far, out, table, charges, tfeat, sfeat, arrived, sent, got
):
    senders, _, cap, _ = src.shape
    slots = senders * cap
    me = lax.axis_index("grp") * inner + lax.axis_index("dom")
    ones = jnp.ones((8, 128), F32)
    zeros = jnp.zeros((8, 128), F32)
    barrier = pltpu.get_barrier_semaphore()

    def greet(k, carry):
        _, device = peer_of(me, k, senders, inner)
        pl.semaphore_signal(barrier, inc=1, device_id=device, device_id_type=MESH)
        return carry

    lax.fori_loop(1, senders, greet, 0)

    for f in range(18, 21):
        sfeat[8 * f : 8 * f + 8] = ones
    for f in range(24, FEATURES):
        sfeat[8 * f : 8 * f + 8] = zeros
    for u in range(unroll):
        for f in range(21, 24):
            tfeat[u, 8 * f : 8 * f + 8] = ones
        for f in range(24, FEATURES):
            tfeat[u, 8 * f : 8 * f + 8] = zeros

    def prepare(i, carry):
        cross, square = source_features(*(src[i, c] - 1.0 for c in range(3)))
        for f, v in list(enumerate(cross)) + list(enumerate(square, 21)):
            sfeat[8 * f : 8 * f + 8] = v
        for s in range(8):
            table[i * 8 + s] = sfeat[pl.ds(s, FEATURES, stride=8), :].astype(BF16)
        charges[pl.ds(i * 8, 8)] = src[i, 3] * (0.25 / math.pi)
        return carry

    lax.fori_loop(0, senders, prepare, 0)
    pl.semaphore_wait(barrier, senders - 1)

    def send(k):
        peer, device = peer_of(me, k, senders, inner)
        pltpu.make_async_remote_copy(
            src_ref=far.at[peer],
            dst_ref=arrived.at[me],
            send_sem=sent,
            recv_sem=got,
            device_id=device,
            device_id_type=MESH,
        ).start()

    def send_all(k, carry):
        send(k)
        return carry

    lax.fori_loop(1, senders, send_all, 0)
    lane_part = lax.broadcasted_iota(jnp.int32, (128, 128), 1) // FEATURES

    def rows(i, carry):
        for u in range(unroll):
            block = i * unroll + u
            info = src[block, 4]
            place = [
                (info[:, c : c + 1] - 1.0) + HALF * off[c, pl.ds(block * 8, 8), :] for c in range(3)
            ]
            for f, v in enumerate(target_features(*place, SOFT_SQ)):
                tfeat[u, 8 * f : 8 * f + 8] = v
            for s in range(8):
                feat = tfeat[u, pl.ds(s, FEATURES, stride=8), :]
                turned = jnp.concatenate([feat.astype(BF16)] * 4, axis=0).T
                left = jnp.concatenate(
                    [jnp.where(lane_part == k, turned, jnp.zeros_like(turned)) for k in range(4)],
                    axis=0,
                )
                at = [near_list[j * slots + block * 8 + s] for j in range(8)]
                right = jnp.concatenate(
                    [
                        jnp.concatenate([table[at[2 * k]], table[at[2 * k + 1]]], axis=1)
                        for k in range(4)
                    ],
                    axis=0,
                )
                dist_sq = jnp.dot(left, right, preferred_element_type=F32)
                total = None
                for k in range(4):
                    for h in range(2):
                        weight = charges[pl.ds(at[2 * k + h], 1), :]
                        part = dist_sq[128 * k : 128 * k + 128, 128 * h : 128 * h + 128]
                        term = lax.rsqrt(part) * weight
                        total = term if total is None else total + term
                out[pl.ds(block * 8 + s, 1), :] = jnp.sum(total.T, axis=0, keepdims=True)
            live = info[:, 3:4] > 0.5
            out[pl.ds(block * 8, 8), :] = jnp.where(live, out[pl.ds(block * 8, 8), :], 0.0)
        return carry

    lax.fori_loop(0, senders // unroll, rows, 0)

    everything = pltpu.make_async_remote_copy(
        src_ref=far.at[pl.ds(0, senders - 1)],
        dst_ref=arrived.at[pl.ds(0, senders - 1)],
        send_sem=sent,
        recv_sem=got,
        device_id=peer_of(me, 1, senders, inner)[1],
        device_id_type=MESH,
    )
    everything.wait_send()
    everything.wait_recv()
    arrived[me] = far[me]

    def add(i, carry):
        out[pl.ds(i * 8, 8), :] += arrived[i]
        return carry

    lax.fori_loop(0, senders, add, 0, unroll=8)


def near_field(src, offsets, near_list, far, inner, unroll=8):
    senders, _, cap, _ = src.shape
    slots = senders * cap
    vmem = pl.BlockSpec(memory_space=pltpu.VMEM)
    return pl.pallas_call(
        functools.partial(near_kernel, unroll, inner),
        out_shape=jax.ShapeDtypeStruct((slots, 128), F32),
        in_specs=[pl.BlockSpec(memory_space=pltpu.SMEM), vmem, vmem, vmem],
        out_specs=vmem,
        scratch_shapes=[
            pltpu.VMEM((slots, FEATURES, 128), BF16),
            pltpu.VMEM((slots, 128), F32),
            pltpu.VMEM((unroll, FEATURES * 8, 128), F32),
            pltpu.VMEM((FEATURES * 8, 128), F32),
            pltpu.VMEM((senders, cap, 128), F32),
            pltpu.SemaphoreType.DMA,
            pltpu.SemaphoreType.DMA,
        ],
        compiler_params=pltpu.CompilerParams(
            vmem_limit_bytes=28 << 20, collective_id=0, has_side_effects=True
        ),
        cost_estimate=pl.CostEstimate(
            flops=2 * slots * 512 * 128 * 256, bytes_accessed=8 << 20, transcendentals=slots << 17
        ),
        name="near_field",
    )(near_list, src, offsets, far)


def surface_weights():
    grid = np.linspace(-1.0, 1.0, ORDER)
    points = np.stack(np.meshgrid(grid, grid, grid, indexing="ij"), 0).reshape(3, -1)
    on_surface = np.max(np.abs(points), axis=0) > 1.0 - 1e-09
    points = (points[:, on_surface] * RADIUS).astype(np.float32)
    fill = 320 - points.shape[1]
    points = np.concatenate([points, np.repeat(points[:, :1], fill, axis=1)], axis=1)

    def split(v):
        high = v.astype(ml_dtypes.bfloat16).astype(np.float32)
        rest = v - high
        middle = rest.astype(ml_dtypes.bfloat16).astype(np.float32)
        return high, middle, rest - middle

    rows = []
    for c in range(3):
        h, m, l = split(-2.0 * points[c])
        rows += [h, m, l, h, m, h]
    rows += [np.ones(320, np.float32)] * 3
    rows += list(split(np.sum(points * points, axis=0)))
    rows += [np.zeros(320, np.float32)] * (FEATURES - len(rows))
    rows = np.stack(rows)
    main = np.repeat(rows[:, :256], 8, axis=0)
    last = np.zeros((FEATURES, 8, 512), np.float32)
    for s in range(8):
        last[:, s, 64 * s : 64 * s + 64] = rows[:, 256:]
    last = last.reshape(FEATURES * 8, 512)
    return main.astype(ml_dtypes.bfloat16), last.astype(ml_dtypes.bfloat16)


def far_rows(unroll, dest, off, dens, main, last, out, tfeat, shift):
    ones = jnp.ones((8, 128), F32)
    zeros = jnp.zeros((8, 128), F32)
    for u in range(unroll):
        for f in range(21, 24):
            tfeat[u, 8 * f : 8 * f + 8] = ones
        for f in range(24, FEATURES):
            tfeat[u, 8 * f : 8 * f + 8] = zeros
    row_of_lane = lax.broadcasted_iota(jnp.int32, (128, 8 * FEATURES), 1) % 8
    low_half = lax.broadcasted_iota(jnp.int32, (1, 128), 1) < 64

    def rows(i, carry):
        for u in range(unroll):
            first = (i * unroll + u) * 8
            at = [dest[first + t] for t in range(8)]
            for t in range(8):
                for c in range(3):
                    shift[u, c, t : t + 1, :] = off[at[t] // 8, c, pl.ds(at[t] % 8, 1), :]
            for f, v in enumerate(target_features(*(shift[u, c] for c in range(3)), 0.0)):
                tfeat[u, 8 * f : 8 * f + 8] = v
            turned = tfeat[u].astype(BF16).T
            weights = [dens[pl.ds(first + t, 1), :] for t in range(8)]
            tail_sq = jnp.dot(turned, last[...], preferred_element_type=F32)
            for p in range(4):
                pair = jnp.where(
                    low_half,
                    weights[2 * p][:, 256:384],
                    pltpu.roll(weights[2 * p + 1][:, 256:384], 64, 1),
                )
                tail = lax.rsqrt(tail_sq[:, 128 * p : 128 * p + 128]) * pair
                for h in range(2):
                    t = 2 * p + h
                    left = jnp.where(row_of_lane == t, turned, jnp.zeros_like(turned))
                    dist_sq = jnp.dot(left, main[...], preferred_element_type=F32)
                    total = lax.rsqrt(dist_sq[:, :128]) * weights[t][:, :128]
                    total = total + lax.rsqrt(dist_sq[:, 128:]) * weights[t][:, 128:256]
                    total = total + jnp.where(low_half == (h == 0), tail, 0.0)
                    line = jnp.sum(total.T, axis=0, keepdims=True)
                    out[pl.ds(first + t, 1), :] = line * (0.25 / (math.pi * HALF))
        return carry

    lax.fori_loop(0, dens.shape[0] // (8 * unroll), rows, 0)


def exchange_kernel(
    unroll, inner,
    which, dest, slot_leaf, packed, offsets, rim, own, ops, m2l, main, last,
    received, leaf, far,
    stacked, dens, at_leaves, lines, tfeat, shift, off_sent, off_got, src_sent, src_got,
):
    devices, _, cap, points = packed.shape
    leaves, width = m2l.shape
    me = lax.axis_index("grp") * inner + lax.axis_index("dom")
    barrier = pltpu.get_barrier_semaphore()

    def greet(k, carry):
        _, device = peer_of(me, k, devices, inner)
        pl.semaphore_signal(barrier, inc=1, device_id=device, device_id_type=MESH)
        return carry

    lax.fori_loop(1, devices, greet, 0)
    pl.semaphore_wait(barrier, devices - 1)

    def send_offsets(k, carry):
        peer, device = peer_of(me, k, devices, inner)
        pltpu.make_async_remote_copy(
            src_ref=offsets.at[:, pl.ds(peer * cap, cap), :],
            dst_ref=at_leaves.at[me],
            send_sem=off_sent,
            recv_sem=off_got,
            device_id=device,
            device_id_type=MESH,
        ).start()
        return carry

    lax.fori_loop(1, devices, send_offsets, 0)

    def send_sources(k, carry):
        peer, device = peer_of(me, k, devices, inner)
        pltpu.make_async_remote_copy(
            src_ref=packed.at[peer],
            dst_ref=received.at[me],
            send_sem=src_sent,
            recv_sem=src_got,
            device_id=device,
            device_id_type=MESH,
        ).start()
        return carry

    lax.fori_loop(1, devices, send_sources, 0)
    at_leaves[me] = offsets[:, pl.ds(me * cap, cap), :]
    received[me] = packed[me]

    parents = jnp.concatenate([rim[...], own[...]], axis=0)
    count = parents.shape[0]
    for o in range(ops.shape[0]):
        stacked[o * count : (o + 1) * count, :] = lax.dot_general(
            parents,
            ops[o],
            (((1,), (1,)), ((), ())),
            precision=lax.Precision.HIGHEST,
            preferred_element_type=F32,
        )
    dens[...] = jnp.zeros_like(dens)
    lines[leaves:, :] = jnp.zeros((8, points), F32)

    def place(j, carry):
        row = m2l[pl.ds(j, 1), :] + stacked[pl.ds(which[j], 1), :]
        leaf[pl.ds(j, 1), :] = row
        dens[pl.ds(j, 1), 0:width] = row
        return carry

    lax.fori_loop(0, leaves, place, 0, unroll=8)

    def all_of(ref, sent, got):
        return pltpu.make_async_remote_copy(
            src_ref=ref.at[pl.ds(0, devices - 1)],
            dst_ref=ref.at[pl.ds(0, devices - 1)],
            send_sem=sent,
            recv_sem=got,
            device_id=peer_of(me, 1, devices, inner)[1],
            device_id_type=MESH,
        )

    all_of(at_leaves, off_sent, off_got).wait_recv()
    far_rows(unroll, dest, at_leaves, dens, main, last, lines, tfeat, shift)

    def to_slots(i, carry):
        for k in range(cap):
            far[i, k : k + 1, :] = lines[pl.ds(slot_leaf[i * cap + k], 1), :]
        return carry

    lax.fori_loop(0, devices, to_slots, 0, unroll=2)
    all_of(received, src_sent, src_got).wait_recv()
    all_of(at_leaves, off_sent, off_got).wait_send()
    all_of(received, src_sent, src_got).wait_send()


def exchange(which, dest, slot_leaf, packed, offsets, rim, own, ops, m2l, inner, unroll=4):
    devices, _, cap, points = packed.shape
    leaves, width = m2l.shape
    count = rim.shape[0] + own.shape[0]
    main, last = surface_weights()
    vmem = pl.BlockSpec(memory_space=pltpu.VMEM)
    smem = pl.BlockSpec(memory_space=pltpu.SMEM)
    return pl.pallas_call(
        functools.partial(exchange_kernel, unroll, inner),
        out_shape=(
            jax.ShapeDtypeStruct(packed.shape, F32),
            jax.ShapeDtypeStruct((leaves, width), F32),
            jax.ShapeDtypeStruct((devices, cap, points), F32),
        ),
        in_specs=[smem] * 3 + [vmem] * 8,
        out_specs=(vmem, vmem, vmem),
        scratch_shapes=[
            pltpu.VMEM((ops.shape[0] * count, width), F32),
            pltpu.VMEM((leaves, 384), F32),
            pltpu.VMEM((devices, 3, cap, points), F32),
            pltpu.VMEM((leaves + 8, points), F32),
            pltpu.VMEM((unroll, FEATURES * 8, 128), F32),
            pltpu.VMEM((unroll, 3, 8, 128), F32),
        ]
        + [pltpu.SemaphoreType.DMA] * 4,
        compiler_params=pltpu.CompilerParams(
            vmem_limit_bytes=28 << 20, collective_id=1, has_side_effects=True
        ),
        name="exchange",
    )(
        which, dest, slot_leaf, packed, offsets, rim, own, ops, m2l,
        jnp.asarray(main), jnp.asarray(last),
    )


def on_device(
    parent_local,
    parent_slot,
    child_octant,
    child_m2l,
    l2l_ops,
    leaf_center,
    src_coords,
    src_charge,
    obs_owner,
    obs_offset,
    near_slots,
):
    devices = lax.axis_size(AXES)
    leaf_dev, width = child_m2l.shape
    slots, _, points = obs_offset.shape
    cap = slots // devices
    me = lax.axis_index(AXES)
    mine = lax.dynamic_slice_in_dim(obs_owner, me * leaf_dev, leaf_dev)

    rim = from_behind(parent_local[parent_local.shape[0] - RIM :], AXES, 1)
    packed, dest, slot_leaf = pack(
        mine, jnp.transpose(src_coords, (1, 0, 2)), src_charge, leaf_center, devices, cap
    )
    which = child_octant * (RIM + parent_local.shape[0]) + parent_slot
    offsets = jnp.transpose(obs_offset, (1, 0, 2))
    inner = lax.axis_size("dom")
    received, leaf_local, far = exchange(
        which, dest, slot_leaf, packed, offsets, rim, parent_local, l2l_ops, child_m2l, inner
    )
    near_list = jnp.transpose(near_slots).reshape(-1)
    potential = near_field(received, offsets, near_list, far, inner)
    return (leaf_local, potential)


def solution(mesh):
    placed = (
        P(AXES, None),
        P(AXES),
        P(AXES),
        P(AXES, None),
        P(),
        P(AXES, None),
        P(AXES, None, None),
        P(AXES, None),
        P(),
        P(AXES, None, None),
        P(AXES, None),
    )
    return jax.shard_map(
        on_device,
        mesh=mesh,
        in_specs=placed,
        out_specs=(P(AXES, None), P(AXES, None)),
        check_vma=False,
    )
```

```python
import functools
import math

import jax
import jax.numpy as jnp
import ml_dtypes
import numpy as np
from jax import lax
from jax.experimental import pallas as pl
from jax.experimental.pallas import tpu as pltpu
from jax.sharding import PartitionSpec as P

ORDER = 8
RIM = 16
RADIUS = 2.95
HALF = 0.5
SOFT_SQ = 0.0025
AXES = ("grp", "dom")
F32 = jnp.float32
BF16 = jnp.bfloat16
FEATURES = 32
MESH = pl.DeviceIdType.MESH


def from_behind(block, axis, distance):
    devices = range(lax.axis_size(axis))
    route = [(i - distance, i) for i in devices if i - distance in devices]
    return lax.ppermute(block, axis, route)


def pack_kernel(capacity, owner, coords, charge, center, out, dest, count, tail):
    devices = out.shape[0]
    leaves = charge.shape[0]
    out[...] = jnp.zeros_like(out)
    tail[:, 0:3] = center[...]
    tail[:, 3:4] = jnp.ones((leaves, 1), F32)

    def clear(i, carry):
        count[i] = 0
        return carry

    lax.fori_loop(0, devices, clear, 0, unroll=8)

    def place(j, carry):
        o = owner[j]
        rank = count[o]
        count[o] = rank + 1
        dest[j] = o * capacity + rank
        for c in range(3):
            out[o, c, pl.ds(rank, 1), :] = coords[c, pl.ds(j, 1), :]
        out[o, 3, pl.ds(rank, 1), :] = charge[pl.ds(j, 1), :]
        out[o, 4, pl.ds(rank, 1), 0:4] = tail[pl.ds(j, 1), :]
        return carry

    lax.fori_loop(0, leaves, place, 0, unroll=4)


def pack(owner, coords, charge, center, devices, capacity):
    leaves = charge.shape[0]
    vmem = pl.BlockSpec(memory_space=pltpu.VMEM)
    return pl.pallas_call(
        functools.partial(pack_kernel, capacity),
        out_shape=(
            jax.ShapeDtypeStruct((devices, 5, capacity, 128), F32),
            jax.ShapeDtypeStruct((leaves,), jnp.int32),
        ),
        in_specs=[pl.BlockSpec(memory_space=pltpu.SMEM), vmem, vmem, vmem],
        out_specs=(vmem, pl.BlockSpec(memory_space=pltpu.SMEM)),
        scratch_shapes=[pltpu.SMEM((devices,), jnp.int32), pltpu.VMEM((leaves, 4), F32)],
        compiler_params=pltpu.CompilerParams(vmem_limit_bytes=14 << 20),
        name="pack",
    )(owner, coords, charge, center)


def leaf_kernel(which, stacked, m2l, leaf, dens):
    leaves, width = m2l.shape
    dens[...] = jnp.zeros_like(dens)

    def place(j, carry):
        row = m2l[pl.ds(j, 1), :] + stacked[pl.ds(which[j], 1), :]
        leaf[pl.ds(j, 1), :] = row
        dens[pl.ds(j, 1), 0:width] = row
        return carry

    lax.fori_loop(0, leaves, place, 0, unroll=8)


def leaf_rows(which, stacked, m2l, padded):
    vmem = pl.BlockSpec(memory_space=pltpu.VMEM)
    smem = pl.BlockSpec(memory_space=pltpu.SMEM)
    return pl.pallas_call(
        leaf_kernel,
        out_shape=(
            jax.ShapeDtypeStruct(m2l.shape, F32),
            jax.ShapeDtypeStruct((m2l.shape[0], padded), F32),
        ),
        in_specs=[smem, vmem, vmem],
        out_specs=(vmem, vmem),
        compiler_params=pltpu.CompilerParams(vmem_limit_bytes=14 << 20),
        cost_estimate=pl.CostEstimate(flops=1 << 18, bytes_accessed=8 << 20, transcendentals=0),
        name="leaf_rows",
    )(which, stacked, m2l)


def split3(v):
    high = v.astype(BF16).astype(F32)
    rest = v - high
    middle = rest.astype(BF16).astype(F32)
    return high, middle, rest - middle


def target_features(x, y, z, extra):
    out = []
    for v in (x, y, z):
        h, m, l = split3(v)
        out += [h, h, h, m, m, l]
    return out + list(split3(x * x + y * y + z * z + extra))


def source_features(x, y, z):
    out = []
    for v in (x, y, z):
        h, m, l = split3(-2.0 * v)
        out += [h, m, l, h, m, h]
    return out, list(split3(x * x + y * y + z * z))


def peer_of(me, k, devices, inner):
    peer = lax.rem(me + k, devices)
    return peer, (peer // inner, lax.rem(peer, inner))


def near_kernel(
    unroll, inner, near_list, src, off, far, out, table, charges, tfeat, sfeat, arrived, sent, got
):
    senders, _, cap, _ = src.shape
    slots = senders * cap
    me = lax.axis_index("grp") * inner + lax.axis_index("dom")
    ones = jnp.ones((8, 128), F32)
    zeros = jnp.zeros((8, 128), F32)
    barrier = pltpu.get_barrier_semaphore()

    def greet(k, carry):
        _, device = peer_of(me, k, senders, inner)
        pl.semaphore_signal(barrier, inc=1, device_id=device, device_id_type=MESH)
        return carry

    lax.fori_loop(1, senders, greet, 0)

    for f in range(18, 21):
        sfeat[8 * f : 8 * f + 8] = ones
    for f in range(24, FEATURES):
        sfeat[8 * f : 8 * f + 8] = zeros
    for u in range(unroll):
        for f in range(21, 24):
            tfeat[u, 8 * f : 8 * f + 8] = ones
        for f in range(24, FEATURES):
            tfeat[u, 8 * f : 8 * f + 8] = zeros

    def prepare(i, carry):
        cross, square = source_features(*(src[i, c] - 1.0 for c in range(3)))
        for f, v in list(enumerate(cross)) + list(enumerate(square, 21)):
            sfeat[8 * f : 8 * f + 8] = v
        for s in range(8):
            table[i * 8 + s] = sfeat[pl.ds(s, FEATURES, stride=8), :].astype(BF16)
        charges[pl.ds(i * 8, 8)] = src[i, 3] * (0.25 / math.pi)
        return carry

    lax.fori_loop(0, senders, prepare, 0, unroll=4)
    pl.semaphore_wait(barrier, senders - 1)

    def send(k):
        peer, device = peer_of(me, k, senders, inner)
        pltpu.make_async_remote_copy(
            src_ref=far.at[peer],
            dst_ref=arrived.at[me],
            send_sem=sent,
            recv_sem=got,
            device_id=device,
            device_id_type=MESH,
        ).start()

    def send_all(k, carry):
        send(k)
        return carry

    lax.fori_loop(1, senders, send_all, 0)
    lane_part = lax.broadcasted_iota(jnp.int32, (128, 128), 1) // FEATURES

    def rows(i, carry):
        for u in range(unroll):
            block = i * unroll + u
            info = src[block, 4]
            place = [
                (info[:, c : c + 1] - 1.0) + HALF * off[c, pl.ds(block * 8, 8), :] for c in range(3)
            ]
            for f, v in enumerate(target_features(*place, SOFT_SQ)):
                tfeat[u, 8 * f : 8 * f + 8] = v
            for s in range(8):
                feat = tfeat[u, pl.ds(s, FEATURES, stride=8), :]
                turned = jnp.concatenate([feat.astype(BF16)] * 4, axis=0).T
                left = jnp.concatenate(
                    [jnp.where(lane_part == k, turned, jnp.zeros_like(turned)) for k in range(4)],
                    axis=0,
                )
                at = [near_list[j * slots + block * 8 + s] for j in range(8)]
                right = jnp.concatenate(
                    [
                        jnp.concatenate([table[at[2 * k]], table[at[2 * k + 1]]], axis=1)
                        for k in range(4)
                    ],
                    axis=0,
                )
                dist_sq = jnp.dot(left, right, preferred_element_type=F32)
                total = None
                for k in range(4):
                    for h in range(2):
                        weight = charges[pl.ds(at[2 * k + h], 1), :]
                        part = dist_sq[128 * k : 128 * k + 128, 128 * h : 128 * h + 128]
                        term = lax.rsqrt(part) * weight
                        total = term if total is None else total + term
                out[pl.ds(block * 8 + s, 1), :] = jnp.sum(total.T, axis=0, keepdims=True)
            live = info[:, 3:4] > 0.5
            out[pl.ds(block * 8, 8), :] = jnp.where(live, out[pl.ds(block * 8, 8), :], 0.0)
        return carry

    lax.fori_loop(0, senders // unroll, rows, 0)

    everything = pltpu.make_async_remote_copy(
        src_ref=far.at[pl.ds(0, senders - 1)],
        dst_ref=arrived.at[pl.ds(0, senders - 1)],
        send_sem=sent,
        recv_sem=got,
        device_id=peer_of(me, 1, senders, inner)[1],
        device_id_type=MESH,
    )
    everything.wait_send()
    everything.wait_recv()
    arrived[me] = far[me]

    def add(i, carry):
        out[pl.ds(i * 8, 8), :] += arrived[i]
        return carry

    lax.fori_loop(0, senders, add, 0, unroll=8)


def near_field(src, offsets, near_list, far, inner, unroll=16):
    senders, _, cap, _ = src.shape
    slots = senders * cap
    vmem = pl.BlockSpec(memory_space=pltpu.VMEM)
    return pl.pallas_call(
        functools.partial(near_kernel, unroll, inner),
        out_shape=jax.ShapeDtypeStruct((slots, 128), F32),
        in_specs=[pl.BlockSpec(memory_space=pltpu.SMEM), vmem, vmem, vmem],
        out_specs=vmem,
        scratch_shapes=[
            pltpu.VMEM((slots, FEATURES, 128), BF16),
            pltpu.VMEM((slots, 128), F32),
            pltpu.VMEM((unroll, FEATURES * 8, 128), F32),
            pltpu.VMEM((FEATURES * 8, 128), F32),
            pltpu.VMEM((senders, cap, 128), F32),
            pltpu.SemaphoreType.DMA,
            pltpu.SemaphoreType.DMA,
        ],
        compiler_params=pltpu.CompilerParams(
            vmem_limit_bytes=28 << 20, collective_id=0, has_side_effects=True
        ),
        cost_estimate=pl.CostEstimate(
            flops=2 * slots * 512 * 128 * 256, bytes_accessed=8 << 20, transcendentals=slots << 17
        ),
        name="near_field",
    )(near_list, src, offsets, far)


def surface_weights():
    grid = np.linspace(-1.0, 1.0, ORDER)
    points = np.stack(np.meshgrid(grid, grid, grid, indexing="ij"), 0).reshape(3, -1)
    on_surface = np.max(np.abs(points), axis=0) > 1.0 - 1e-09
    points = (points[:, on_surface] * RADIUS).astype(np.float32)
    fill = 320 - points.shape[1]
    points = np.concatenate([points, np.repeat(points[:, :1], fill, axis=1)], axis=1)

    def split(v):
        high = v.astype(ml_dtypes.bfloat16).astype(np.float32)
        rest = v - high
        middle = rest.astype(ml_dtypes.bfloat16).astype(np.float32)
        return high, middle, rest - middle

    rows = []
    for c in range(3):
        h, m, l = split(-2.0 * points[c])
        rows += [h, m, l, h, m, h]
    rows += [np.ones(320, np.float32)] * 3
    rows += list(split(np.sum(points * points, axis=0)))
    rows += [np.zeros(320, np.float32)] * (FEATURES - len(rows))
    rows = np.stack(rows)
    main = np.repeat(rows[:, :256], 8, axis=0)
    last = np.zeros((FEATURES, 8, 512), np.float32)
    for s in range(8):
        last[:, s, 64 * s : 64 * s + 64] = rows[:, 256:]
    last = last.reshape(FEATURES * 8, 512)
    return main.astype(ml_dtypes.bfloat16), last.astype(ml_dtypes.bfloat16)


def far_kernel(unroll, dest, off, dens, main, last, out, tfeat, shift):
    ones = jnp.ones((8, 128), F32)
    zeros = jnp.zeros((8, 128), F32)
    out[...] = jnp.zeros_like(out)
    for u in range(unroll):
        for f in range(21, 24):
            tfeat[u, 8 * f : 8 * f + 8] = ones
        for f in range(24, FEATURES):
            tfeat[u, 8 * f : 8 * f + 8] = zeros
    row_of_lane = lax.broadcasted_iota(jnp.int32, (128, 8 * FEATURES), 1) % 8
    low_half = lax.broadcasted_iota(jnp.int32, (1, 128), 1) < 64

    def rows(i, carry):
        for u in range(unroll):
            first = (i * unroll + u) * 8
            at = [dest[first + t] for t in range(8)]
            for t in range(8):
                for c in range(3):
                    shift[u, c, t : t + 1, :] = off[at[t] // 8, c, pl.ds(at[t] % 8, 1), :]
            for f, v in enumerate(target_features(*(shift[u, c] for c in range(3)), 0.0)):
                tfeat[u, 8 * f : 8 * f + 8] = v
            turned = tfeat[u].astype(BF16).T
            weights = [dens[pl.ds(first + t, 1), :] for t in range(8)]
            tail_sq = jnp.dot(turned, last[...], preferred_element_type=F32)
            for p in range(4):
                pair = jnp.where(
                    low_half,
                    weights[2 * p][:, 256:384],
                    pltpu.roll(weights[2 * p + 1][:, 256:384], 64, 1),
                )
                tail = lax.rsqrt(tail_sq[:, 128 * p : 128 * p + 128]) * pair
                for h in range(2):
                    t = 2 * p + h
                    left = jnp.where(row_of_lane == t, turned, jnp.zeros_like(turned))
                    dist_sq = jnp.dot(left, main[...], preferred_element_type=F32)
                    total = lax.rsqrt(dist_sq[:, :128]) * weights[t][:, :128]
                    total = total + lax.rsqrt(dist_sq[:, 128:]) * weights[t][:, 128:256]
                    total = total + jnp.where(low_half == (h == 0), tail, 0.0)
                    line = jnp.sum(total.T, axis=0, keepdims=True)
                    out[pl.ds(at[t], 1), :] = line * (0.25 / (math.pi * HALF))
        return carry

    lax.fori_loop(0, dens.shape[0] // (8 * unroll), rows, 0)


def far_field(dest, offsets, dens, unroll=4):
    devices, _, cap, points = offsets.shape
    main, last = surface_weights()
    vmem = pl.BlockSpec(memory_space=pltpu.VMEM)
    return pl.pallas_call(
        functools.partial(far_kernel, unroll),
        out_shape=jax.ShapeDtypeStruct((devices * cap, points), F32),
        in_specs=[pl.BlockSpec(memory_space=pltpu.SMEM)] + [vmem] * 4,
        out_specs=vmem,
        scratch_shapes=[
            pltpu.VMEM((unroll, FEATURES * 8, 128), F32),
            pltpu.VMEM((unroll, 3, 8, 128), F32),
        ],
        compiler_params=pltpu.CompilerParams(vmem_limit_bytes=14 << 20),
        cost_estimate=pl.CostEstimate(
            flops=2 * dens.shape[0] * 128 * 256 * 384,
            bytes_accessed=4 << 20,
            transcendentals=dens.shape[0] * 128 * 320,
        ),
        name="far_field",
    )(dest, offsets, dens, jnp.asarray(main), jnp.asarray(last))


def on_device(
    parent_local,
    parent_slot,
    child_octant,
    child_m2l,
    l2l_ops,
    leaf_center,
    src_coords,
    src_charge,
    obs_owner,
    obs_offset,
    near_slots,
):
    devices = lax.axis_size(AXES)
    leaf_dev, width = child_m2l.shape
    slots, _, points = obs_offset.shape
    cap = slots // devices
    me = lax.axis_index(AXES)
    mine = lax.dynamic_slice_in_dim(obs_owner, me * leaf_dev, leaf_dev)

    rim = from_behind(parent_local[parent_local.shape[0] - RIM :], AXES, 1)
    packed, dest = pack(mine, jnp.transpose(src_coords, (1, 0, 2)), src_charge, leaf_center, devices, cap)

    offsets = jnp.transpose(obs_offset, (1, 0, 2))
    outgoing = jnp.transpose(offsets.reshape(3, devices, cap, points), (1, 0, 2, 3))
    outgoing, rim = lax.optimization_barrier((outgoing, rim))
    at_leaves = lax.all_to_all(outgoing, AXES, 0, 0, tiled=True)

    parents = jnp.concatenate([rim, parent_local], axis=0)
    moved = jnp.einsum("pr,oqr->opq", parents, l2l_ops, precision=lax.Precision.HIGHEST)
    stacked = moved.reshape(l2l_ops.shape[0] * parents.shape[0], width)
    which = child_octant * parents.shape[0] + parent_slot
    leaf_local, dens = leaf_rows(which, stacked, child_m2l, 384)
    packed, dens = lax.optimization_barrier((packed, dens))
    received = lax.all_to_all(packed, AXES, 0, 0, tiled=True)
    far = far_field(dest, at_leaves, dens)
    far = far.reshape(devices, cap, points)
    near_list = jnp.transpose(near_slots).reshape(-1)
    potential = near_field(received, offsets, near_list, far, lax.axis_size("dom"))
    return (leaf_local, potential)


def solution(mesh):
    placed = (
        P(AXES, None),
        P(AXES),
        P(AXES),
        P(AXES, None),
        P(),
        P(AXES, None),
        P(AXES, None, None),
        P(AXES, None),
        P(),
        P(AXES, None, None),
        P(AXES, None),
    )
    return jax.shard_map(
        on_device,
        mesh=mesh,
        in_specs=placed,
        out_specs=(P(AXES, None), P(AXES, None)),
        check_vma=False,
    )
```

```python
import functools
import math

import jax
import jax.numpy as jnp
import ml_dtypes
import numpy as np
from jax import lax
from jax.experimental import pallas as pl
from jax.experimental.pallas import tpu as pltpu
from jax.sharding import PartitionSpec as P

ORDER = 8
RIM = 16
RADIUS = 2.95
HALF = 0.5
SOFT_SQ = 0.0025
AXES = ("grp", "dom")
F32 = jnp.float32
BF16 = jnp.bfloat16
FEATURES = 32
MESH = pl.DeviceIdType.MESH


def from_behind(block, axis, distance):
    devices = range(lax.axis_size(axis))
    route = [(i - distance, i) for i in devices if i - distance in devices]
    return lax.ppermute(block, axis, route)


def pack_kernel(capacity, owner, coords, charge, center, out, dest, count, tail):
    devices = out.shape[0]
    leaves = charge.shape[0]
    out[...] = jnp.zeros_like(out)
    for h in range(2):
        tail[:, 4 * h : 4 * h + 3] = center[...]
        tail[:, 4 * h + 3 : 4 * h + 4] = jnp.ones((leaves, 1), F32)
    part = lax.broadcasted_iota(jnp.int32, (1, 8), 1) // 4

    def clear(i, carry):
        count[i] = 0
        return carry

    lax.fori_loop(0, devices, clear, 0, unroll=8)

    def place(j, carry):
        o = owner[j]
        rank = count[o]
        count[o] = rank + 1
        dest[j] = o * capacity + rank
        half, row = rank // 4, rank % 4
        for c in range(3):
            out[o, 2 * c + half, pl.ds(row, 1), :] = coords[c, pl.ds(j, 1), :]
        out[o, 6 + half, pl.ds(row, 1), :] = charge[pl.ds(j, 1), :]
        old = out[o, 8, pl.ds(row, 1), 0:8]
        out[o, 8, pl.ds(row, 1), 0:8] = jnp.where(part == half, tail[pl.ds(j, 1), :], old)
        return carry

    lax.fori_loop(0, leaves, place, 0, unroll=4)


def pack(owner, coords, charge, center, devices, capacity):
    leaves = charge.shape[0]
    vmem = pl.BlockSpec(memory_space=pltpu.VMEM)
    return pl.pallas_call(
        functools.partial(pack_kernel, capacity),
        out_shape=(
            jax.ShapeDtypeStruct((devices, 9, capacity // 2, 128), F32),
            jax.ShapeDtypeStruct((leaves,), jnp.int32),
        ),
        in_specs=[pl.BlockSpec(memory_space=pltpu.SMEM), vmem, vmem, vmem],
        out_specs=(vmem, pl.BlockSpec(memory_space=pltpu.SMEM)),
        scratch_shapes=[pltpu.SMEM((devices,), jnp.int32), pltpu.VMEM((leaves, 8), F32)],
        compiler_params=pltpu.CompilerParams(vmem_limit_bytes=14 << 20),
        name="pack",
    )(owner, coords, charge, center)


def leaf_kernel(which, stacked, m2l, leaf, dens):
    leaves, width = m2l.shape
    dens[...] = jnp.zeros_like(dens)

    def place(j, carry):
        row = m2l[pl.ds(j, 1), :] + stacked[pl.ds(which[j], 1), :]
        leaf[pl.ds(j, 1), :] = row
        dens[pl.ds(j, 1), 0:width] = row
        return carry

    lax.fori_loop(0, leaves, place, 0, unroll=8)


def leaf_rows(which, stacked, m2l, padded):
    vmem = pl.BlockSpec(memory_space=pltpu.VMEM)
    smem = pl.BlockSpec(memory_space=pltpu.SMEM)
    return pl.pallas_call(
        leaf_kernel,
        out_shape=(
            jax.ShapeDtypeStruct(m2l.shape, F32),
            jax.ShapeDtypeStruct((m2l.shape[0], padded), F32),
        ),
        in_specs=[smem, vmem, vmem],
        out_specs=(vmem, vmem),
        compiler_params=pltpu.CompilerParams(vmem_limit_bytes=14 << 20),
        cost_estimate=pl.CostEstimate(flops=1 << 18, bytes_accessed=8 << 20, transcendentals=0),
        name="leaf_rows",
    )(which, stacked, m2l)


def split3(v):
    high = v.astype(BF16).astype(F32)
    rest = v - high
    middle = rest.astype(BF16).astype(F32)
    return high, middle, rest - middle


def target_features(x, y, z, extra):
    out = []
    for v in (x, y, z):
        h, m, l = split3(v)
        out += [h, h, h, m, m, l]
    return out + list(split3(x * x + y * y + z * z + extra))


def source_features(x, y, z):
    out = []
    for v in (x, y, z):
        h, m, l = split3(-2.0 * v)
        out += [h, m, l, h, m, h]
    return out, list(split3(x * x + y * y + z * z))


def peer_of(me, k, devices, inner):
    peer = lax.rem(me + k, devices)
    return peer, (peer // inner, lax.rem(peer, inner))


def both_halves(src, i, c):
    return jnp.concatenate([src[i, 2 * c], src[i, 2 * c + 1]], axis=0)


def near_kernel(
    unroll, inner, near_list, src, off, far, out, table, charges, tfeat, sfeat, arrived, sent, got
):
    senders, _, cap, _ = src.shape
    cap = 2 * cap
    slots = senders * cap
    me = lax.axis_index("grp") * inner + lax.axis_index("dom")
    ones = jnp.ones((8, 128), F32)
    zeros = jnp.zeros((8, 128), F32)
    barrier = pltpu.get_barrier_semaphore()

    def greet(k, carry):
        _, device = peer_of(me, k, senders, inner)
        pl.semaphore_signal(barrier, inc=1, device_id=device, device_id_type=MESH)
        return carry

    lax.fori_loop(1, senders, greet, 0)

    for f in range(18, 21):
        sfeat[8 * f : 8 * f + 8] = ones
    for f in range(24, FEATURES):
        sfeat[8 * f : 8 * f + 8] = zeros
    for u in range(unroll):
        for f in range(21, 24):
            tfeat[u, 8 * f : 8 * f + 8] = ones
        for f in range(24, FEATURES):
            tfeat[u, 8 * f : 8 * f + 8] = zeros

    def prepare(i, carry):
        cross, square = source_features(
            *(both_halves(src, i, c) - 1.0 for c in range(3))
        )
        for f, v in list(enumerate(cross)) + list(enumerate(square, 21)):
            sfeat[8 * f : 8 * f + 8] = v
        for s in range(8):
            table[i * 8 + s] = sfeat[pl.ds(s, FEATURES, stride=8), :].astype(BF16)
        charges[pl.ds(i * 8, 8)] = both_halves(src, i, 3) * (0.25 / math.pi)
        return carry

    lax.fori_loop(0, senders, prepare, 0, unroll=4)
    pl.semaphore_wait(barrier, senders - 1)

    def send(k):
        peer, device = peer_of(me, k, senders, inner)
        pltpu.make_async_remote_copy(
            src_ref=far.at[peer],
            dst_ref=arrived.at[me],
            send_sem=sent,
            recv_sem=got,
            device_id=device,
            device_id_type=MESH,
        ).start()

    def send_all(k, carry):
        send(k)
        return carry

    lax.fori_loop(1, senders, send_all, 0)
    lane_part = lax.broadcasted_iota(jnp.int32, (128, 128), 1) // FEATURES

    def rows(i, carry):
        for u in range(unroll):
            block = i * unroll + u
            info = src[block, 8]
            info = jnp.concatenate([info[:, 0:4], info[:, 4:8]], axis=0)
            place = [
                (info[:, c : c + 1] - 1.0) + HALF * off[c, pl.ds(block * 8, 8), :] for c in range(3)
            ]
            for f, v in enumerate(target_features(*place, SOFT_SQ)):
                tfeat[u, 8 * f : 8 * f + 8] = v
            for s in range(8):
                feat = tfeat[u, pl.ds(s, FEATURES, stride=8), :]
                turned = jnp.concatenate([feat.astype(BF16)] * 4, axis=0).T
                left = jnp.concatenate(
                    [jnp.where(lane_part == k, turned, jnp.zeros_like(turned)) for k in range(4)],
                    axis=0,
                )
                at = [near_list[j * slots + block * 8 + s] for j in range(8)]
                right = jnp.concatenate(
                    [
                        jnp.concatenate([table[at[2 * k]], table[at[2 * k + 1]]], axis=1)
                        for k in range(4)
                    ],
                    axis=0,
                )
                dist_sq = jnp.dot(left, right, preferred_element_type=F32)
                total = None
                for k in range(4):
                    for h in range(2):
                        weight = charges[pl.ds(at[2 * k + h], 1), :]
                        part = dist_sq[128 * k : 128 * k + 128, 128 * h : 128 * h + 128]
                        term = lax.rsqrt(part) * weight
                        total = term if total is None else total + term
                out[pl.ds(block * 8 + s, 1), :] = jnp.sum(total.T, axis=0, keepdims=True)
            live = info[:, 3:4] > 0.5
            out[pl.ds(block * 8, 8), :] = jnp.where(live, out[pl.ds(block * 8, 8), :], 0.0)
        return carry

    lax.fori_loop(0, senders // unroll, rows, 0)

    everything = pltpu.make_async_remote_copy(
        src_ref=far.at[pl.ds(0, senders - 1)],
        dst_ref=arrived.at[pl.ds(0, senders - 1)],
        send_sem=sent,
        recv_sem=got,
        device_id=peer_of(me, 1, senders, inner)[1],
        device_id_type=MESH,
    )
    everything.wait_send()
    everything.wait_recv()
    arrived[me] = far[me]

    def add(i, carry):
        out[pl.ds(i * 8, 8), :] += arrived[i]
        return carry

    lax.fori_loop(0, senders, add, 0, unroll=8)


def near_field(src, offsets, near_list, far, inner, unroll=16):
    senders, cap, _ = far.shape
    slots = senders * cap
    vmem = pl.BlockSpec(memory_space=pltpu.VMEM)
    return pl.pallas_call(
        functools.partial(near_kernel, unroll, inner),
        out_shape=jax.ShapeDtypeStruct((slots, 128), F32),
        in_specs=[pl.BlockSpec(memory_space=pltpu.SMEM), vmem, vmem, vmem],
        out_specs=vmem,
        scratch_shapes=[
            pltpu.VMEM((slots, FEATURES, 128), BF16),
            pltpu.VMEM((slots, 128), F32),
            pltpu.VMEM((unroll, FEATURES * 8, 128), F32),
            pltpu.VMEM((FEATURES * 8, 128), F32),
            pltpu.VMEM((senders, cap, 128), F32),
            pltpu.SemaphoreType.DMA,
            pltpu.SemaphoreType.DMA,
        ],
        compiler_params=pltpu.CompilerParams(
            vmem_limit_bytes=28 << 20, collective_id=0, has_side_effects=True
        ),
        cost_estimate=pl.CostEstimate(
            flops=2 * slots * 512 * 128 * 256, bytes_accessed=8 << 20, transcendentals=slots << 17
        ),
        name="near_field",
    )(near_list, src, offsets, far)


def surface_weights():
    grid = np.linspace(-1.0, 1.0, ORDER)
    points = np.stack(np.meshgrid(grid, grid, grid, indexing="ij"), 0).reshape(3, -1)
    on_surface = np.max(np.abs(points), axis=0) > 1.0 - 1e-09
    points = (points[:, on_surface] * RADIUS).astype(np.float32)
    fill = 320 - points.shape[1]
    points = np.concatenate([points, np.repeat(points[:, :1], fill, axis=1)], axis=1)

    def split(v):
        high = v.astype(ml_dtypes.bfloat16).astype(np.float32)
        rest = v - high
        middle = rest.astype(ml_dtypes.bfloat16).astype(np.float32)
        return high, middle, rest - middle

    rows = []
    for c in range(3):
        h, m, l = split(-2.0 * points[c])
        rows += [h, m, l, h, m, h]
    rows += [np.ones(320, np.float32)] * 3
    rows += list(split(np.sum(points * points, axis=0)))
    rows += [np.zeros(320, np.float32)] * (FEATURES - len(rows))
    rows = np.stack(rows)
    main = np.repeat(rows[:, :256], 8, axis=0)
    last = np.zeros((FEATURES, 8, 512), np.float32)
    for s in range(8):
        last[:, s, 64 * s : 64 * s + 64] = rows[:, 256:]
    last = last.reshape(FEATURES * 8, 512)
    return main.astype(ml_dtypes.bfloat16), last.astype(ml_dtypes.bfloat16)


def far_kernel(unroll, dest, off, dens, main, last, out, tfeat, shift):
    ones = jnp.ones((8, 128), F32)
    zeros = jnp.zeros((8, 128), F32)
    out[...] = jnp.zeros_like(out)
    for u in range(unroll):
        for f in range(21, 24):
            tfeat[u, 8 * f : 8 * f + 8] = ones
        for f in range(24, FEATURES):
            tfeat[u, 8 * f : 8 * f + 8] = zeros
    row_of_lane = lax.broadcasted_iota(jnp.int32, (128, 8 * FEATURES), 1) % 8
    low_half = lax.broadcasted_iota(jnp.int32, (1, 128), 1) < 64

    def rows(i, carry):
        for u in range(unroll):
            first = (i * unroll + u) * 8
            at = [dest[first + t] for t in range(8)]
            for t in range(8):
                for c in range(3):
                    shift[u, c, t : t + 1, :] = off[at[t] // 8, c, pl.ds(at[t] % 8, 1), :]
            for f, v in enumerate(target_features(*(shift[u, c] for c in range(3)), 0.0)):
                tfeat[u, 8 * f : 8 * f + 8] = v
            turned = tfeat[u].astype(BF16).T
            weights = [dens[pl.ds(first + t, 1), :] for t in range(8)]
            tail_sq = jnp.dot(turned, last[...], preferred_element_type=F32)
            for p in range(4):
                pair = jnp.where(
                    low_half,
                    weights[2 * p][:, 256:384],
                    pltpu.roll(weights[2 * p + 1][:, 256:384], 64, 1),
                )
                tail = lax.rsqrt(tail_sq[:, 128 * p : 128 * p + 128]) * pair
                for h in range(2):
                    t = 2 * p + h
                    left = jnp.where(row_of_lane == t, turned, jnp.zeros_like(turned))
                    dist_sq = jnp.dot(left, main[...], preferred_element_type=F32)
                    total = lax.rsqrt(dist_sq[:, :128]) * weights[t][:, :128]
                    total = total + lax.rsqrt(dist_sq[:, 128:]) * weights[t][:, 128:256]
                    total = total + jnp.where(low_half == (h == 0), tail, 0.0)
                    line = jnp.sum(total.T, axis=0, keepdims=True)
                    out[pl.ds(at[t], 1), :] = line * (0.25 / (math.pi * HALF))
        return carry

    lax.fori_loop(0, dens.shape[0] // (8 * unroll), rows, 0)


def far_field(dest, offsets, dens, unroll=4):
    devices, _, cap, points = offsets.shape
    main, last = surface_weights()
    vmem = pl.BlockSpec(memory_space=pltpu.VMEM)
    return pl.pallas_call(
        functools.partial(far_kernel, unroll),
        out_shape=jax.ShapeDtypeStruct((devices * cap, points), F32),
        in_specs=[pl.BlockSpec(memory_space=pltpu.SMEM)] + [vmem] * 4,
        out_specs=vmem,
        scratch_shapes=[
            pltpu.VMEM((unroll, FEATURES * 8, 128), F32),
            pltpu.VMEM((unroll, 3, 8, 128), F32),
        ],
        compiler_params=pltpu.CompilerParams(vmem_limit_bytes=14 << 20),
        cost_estimate=pl.CostEstimate(
            flops=2 * dens.shape[0] * 128 * 256 * 384,
            bytes_accessed=4 << 20,
            transcendentals=dens.shape[0] * 128 * 320,
        ),
        name="far_field",
    )(dest, offsets, dens, jnp.asarray(main), jnp.asarray(last))


def on_device(
    parent_local,
    parent_slot,
    child_octant,
    child_m2l,
    l2l_ops,
    leaf_center,
    src_coords,
    src_charge,
    obs_owner,
    obs_offset,
    near_slots,
):
    devices = lax.axis_size(AXES)
    leaf_dev, width = child_m2l.shape
    slots, _, points = obs_offset.shape
    cap = slots // devices
    me = lax.axis_index(AXES)
    mine = lax.dynamic_slice_in_dim(obs_owner, me * leaf_dev, leaf_dev)

    rim = from_behind(parent_local[parent_local.shape[0] - RIM :], AXES, 1)
    packed, dest = pack(mine, jnp.transpose(src_coords, (1, 0, 2)), src_charge, leaf_center, devices, cap)

    offsets = jnp.transpose(obs_offset, (1, 0, 2))
    outgoing = jnp.transpose(offsets.reshape(3, devices, cap, points), (1, 0, 2, 3))
    outgoing, rim = lax.optimization_barrier((outgoing, rim))
    at_leaves = lax.all_to_all(outgoing, AXES, 0, 0, tiled=True)

    parents = jnp.concatenate([rim, parent_local], axis=0)
    moved = jnp.einsum("pr,oqr->opq", parents, l2l_ops, precision=lax.Precision.HIGHEST)
    stacked = moved.reshape(l2l_ops.shape[0] * parents.shape[0], width)
    which = child_octant * parents.shape[0] + parent_slot
    leaf_local, dens = leaf_rows(which, stacked, child_m2l, 384)
    packed, dens = lax.optimization_barrier((packed, dens))
    received = lax.all_to_all(packed, AXES, 0, 0, tiled=True)
    far = far_field(dest, at_leaves, dens)
    far = far.reshape(devices, cap, points)
    near_list = jnp.transpose(near_slots).reshape(-1)
    potential = near_field(received, offsets, near_list, far, lax.axis_size("dom"))
    return (leaf_local, potential)


def solution(mesh):
    placed = (
        P(AXES, None),
        P(AXES),
        P(AXES),
        P(AXES, None),
        P(),
        P(AXES, None),
        P(AXES, None, None),
        P(AXES, None),
        P(),
        P(AXES, None, None),
        P(AXES, None),
    )
    return jax.shard_map(
        on_device,
        mesh=mesh,
        in_specs=placed,
        out_specs=(P(AXES, None), P(AXES, None)),
        check_vma=False,
    )
```

```python
import functools
import math

import jax
import jax.numpy as jnp
import ml_dtypes
import numpy as np
from jax import lax
from jax.experimental import pallas as pl
from jax.experimental.pallas import tpu as pltpu
from jax.sharding import PartitionSpec as P

ORDER = 8
RIM = 16
RADIUS = 2.95
HALF = 0.5
SOFT_SQ = 0.0025
AXES = ("grp", "dom")
F32 = jnp.float32
BF16 = jnp.bfloat16
FEATURES = 32
MESH = pl.DeviceIdType.MESH


def from_behind(block, axis, distance):
    devices = range(lax.axis_size(axis))
    route = [(i - distance, i) for i in devices if i - distance in devices]
    return lax.ppermute(block, axis, route)


def pack_kernel(capacity, owner, coords, charge, center, out, dest, count, tail, places):
    devices = out.shape[0]
    leaves = charge.shape[0]
    out[...] = jnp.zeros_like(out)
    tail[:, 0:3] = center[...]
    tail[:, 3:4] = jnp.ones((leaves, 1), F32)
    places[...] = jnp.zeros_like(places)

    def clear(i, carry):
        count[i] = 0
        return carry

    lax.fori_loop(0, devices, clear, 0, unroll=8)

    def place(j, carry):
        o = owner[j]
        rank = count[o]
        count[o] = rank + 1
        dest[j] = o * capacity + rank
        half, row = rank >> 2, rank & 3
        for c in range(3):
            out[o, 2 * c + half, pl.ds(row, 1), :] = coords[c, pl.ds(j, 1), :]
        out[o, 6 + half, pl.ds(row, 1), :] = charge[pl.ds(j, 1), :]
        places[o, pl.ds(rank, 1), :] = tail[pl.ds(j, 1), :]
        return carry

    lax.fori_loop(0, leaves, place, 0, unroll=4)

    def fold(o, carry):
        out[o, 8, :, 0:4] = places[o, 0:4, :]
        out[o, 8, :, 4:8] = places[o, 4:8, :]
        return carry

    lax.fori_loop(0, devices, fold, 0, unroll=8)


def pack(owner, coords, charge, center, devices, capacity):
    leaves = charge.shape[0]
    vmem = pl.BlockSpec(memory_space=pltpu.VMEM)
    return pl.pallas_call(
        functools.partial(pack_kernel, capacity),
        out_shape=(
            jax.ShapeDtypeStruct((devices, 9, capacity // 2, 128), F32),
            jax.ShapeDtypeStruct((leaves,), jnp.int32),
        ),
        in_specs=[pl.BlockSpec(memory_space=pltpu.SMEM), vmem, vmem, vmem],
        out_specs=(vmem, pl.BlockSpec(memory_space=pltpu.SMEM)),
        scratch_shapes=[pltpu.SMEM((devices,), jnp.int32), pltpu.VMEM((leaves, 4), F32), pltpu.VMEM((devices, 8, 4), F32)],
        compiler_params=pltpu.CompilerParams(vmem_limit_bytes=14 << 20),
        name="pack",
    )(owner, coords, charge, center)


def leaf_kernel(which, stacked, m2l, leaf, dens):
    leaves, width = m2l.shape
    dens[...] = jnp.zeros_like(dens)

    def place(j, carry):
        row = m2l[pl.ds(j, 1), :] + stacked[pl.ds(which[j], 1), :]
        leaf[pl.ds(j, 1), :] = row
        dens[pl.ds(j, 1), 0:width] = row
        return carry

    lax.fori_loop(0, leaves, place, 0, unroll=8)


def leaf_rows(which, stacked, m2l, padded):
    vmem = pl.BlockSpec(memory_space=pltpu.VMEM)
    smem = pl.BlockSpec(memory_space=pltpu.SMEM)
    return pl.pallas_call(
        leaf_kernel,
        out_shape=(
            jax.ShapeDtypeStruct(m2l.shape, F32),
            jax.ShapeDtypeStruct((m2l.shape[0], padded), F32),
        ),
        in_specs=[smem, vmem, vmem],
        out_specs=(vmem, vmem),
        compiler_params=pltpu.CompilerParams(vmem_limit_bytes=14 << 20),
        cost_estimate=pl.CostEstimate(flops=1 << 18, bytes_accessed=8 << 20, transcendentals=0),
        name="leaf_rows",
    )(which, stacked, m2l)


def split3(v):
    high = v.astype(BF16).astype(F32)
    rest = v - high
    middle = rest.astype(BF16).astype(F32)
    return high, middle, rest - middle


def target_features(x, y, z, extra):
    out = []
    for v in (x, y, z):
        h, m, l = split3(v)
        out += [h, h, h, m, m, l]
    return out + list(split3(x * x + y * y + z * z + extra))


def source_features(x, y, z):
    out = []
    for v in (x, y, z):
        h, m, l = split3(-2.0 * v)
        out += [h, m, l, h, m, h]
    return out, list(split3(x * x + y * y + z * z))


def peer_of(me, k, devices, inner):
    peer = lax.rem(me + k, devices)
    return peer, (peer // inner, lax.rem(peer, inner))


def both_halves(src, i, c):
    return jnp.concatenate([src[i, 2 * c], src[i, 2 * c + 1]], axis=0)


def near_kernel(
    unroll, inner, near_list, src, off, far, out, table, charges, tfeat, sfeat, arrived, sent, got
):
    senders, _, cap, _ = src.shape
    cap = 2 * cap
    slots = senders * cap
    me = lax.axis_index("grp") * inner + lax.axis_index("dom")
    ones = jnp.ones((8, 128), F32)
    zeros = jnp.zeros((8, 128), F32)
    barrier = pltpu.get_barrier_semaphore()

    def greet(k, carry):
        _, device = peer_of(me, k, senders, inner)
        pl.semaphore_signal(barrier, inc=1, device_id=device, device_id_type=MESH)
        return carry

    lax.fori_loop(1, senders, greet, 0)

    for f in range(18, 21):
        sfeat[8 * f : 8 * f + 8] = ones
    for f in range(24, FEATURES):
        sfeat[8 * f : 8 * f + 8] = zeros
    for u in range(unroll):
        for f in range(21, 24):
            tfeat[u, 8 * f : 8 * f + 8] = ones
        for f in range(24, FEATURES):
            tfeat[u, 8 * f : 8 * f + 8] = zeros

    def prepare(i, carry):
        cross, square = source_features(
            *(both_halves(src, i, c) - 1.0 for c in range(3))
        )
        for f, v in list(enumerate(cross)) + list(enumerate(square, 21)):
            sfeat[8 * f : 8 * f + 8] = v
        for s in range(8):
            table[i * 8 + s] = sfeat[pl.ds(s, FEATURES, stride=8), :].astype(BF16)
        charges[pl.ds(i * 8, 8)] = both_halves(src, i, 3) * (0.25 / math.pi)
        return carry

    lax.fori_loop(0, senders, prepare, 0, unroll=4)
    pl.semaphore_wait(barrier, senders - 1)

    def send(k):
        peer, device = peer_of(me, k, senders, inner)
        pltpu.make_async_remote_copy(
            src_ref=far.at[peer],
            dst_ref=arrived.at[me],
            send_sem=sent,
            recv_sem=got,
            device_id=device,
            device_id_type=MESH,
        ).start()

    def send_all(k, carry):
        send(k)
        return carry

    lax.fori_loop(1, senders, send_all, 0)
    lane_part = lax.broadcasted_iota(jnp.int32, (128, 128), 1) // FEATURES

    def rows(i, carry):
        for u in range(unroll):
            block = i * unroll + u
            info = src[block, 8]
            info = jnp.concatenate([info[:, 0:4], info[:, 4:8]], axis=0)
            place = [
                (info[:, c : c + 1] - 1.0) + HALF * off[c, pl.ds(block * 8, 8), :] for c in range(3)
            ]
            for f, v in enumerate(target_features(*place, SOFT_SQ)):
                tfeat[u, 8 * f : 8 * f + 8] = v
            for s in range(8):
                feat = tfeat[u, pl.ds(s, FEATURES, stride=8), :]
                turned = jnp.concatenate([feat.astype(BF16)] * 4, axis=0).T
                left = jnp.concatenate(
                    [jnp.where(lane_part == k, turned, jnp.zeros_like(turned)) for k in range(4)],
                    axis=0,
                )
                at = [near_list[j * slots + block * 8 + s] for j in range(8)]
                right = jnp.concatenate(
                    [
                        jnp.concatenate([table[at[2 * k]], table[at[2 * k + 1]]], axis=1)
                        for k in range(4)
                    ],
                    axis=0,
                )
                dist_sq = jnp.dot(left, right, preferred_element_type=F32)
                total = None
                for k in range(4):
                    for h in range(2):
                        weight = charges[pl.ds(at[2 * k + h], 1), :]
                        part = dist_sq[128 * k : 128 * k + 128, 128 * h : 128 * h + 128]
                        term = lax.rsqrt(part) * weight
                        total = term if total is None else total + term
                out[pl.ds(block * 8 + s, 1), :] = jnp.sum(total.T, axis=0, keepdims=True)
            live = info[:, 3:4] > 0.5
            out[pl.ds(block * 8, 8), :] = jnp.where(live, out[pl.ds(block * 8, 8), :], 0.0)
        return carry

    lax.fori_loop(0, senders // unroll, rows, 0)

    everything = pltpu.make_async_remote_copy(
        src_ref=far.at[pl.ds(0, senders - 1)],
        dst_ref=arrived.at[pl.ds(0, senders - 1)],
        send_sem=sent,
        recv_sem=got,
        device_id=peer_of(me, 1, senders, inner)[1],
        device_id_type=MESH,
    )
    everything.wait_send()
    everything.wait_recv()
    arrived[me] = far[me]

    def add(i, carry):
        out[pl.ds(i * 8, 8), :] += arrived[i]
        return carry

    lax.fori_loop(0, senders, add, 0, unroll=8)


def near_field(src, offsets, near_list, far, inner, unroll=16):
    senders, cap, _ = far.shape
    slots = senders * cap
    vmem = pl.BlockSpec(memory_space=pltpu.VMEM)
    return pl.pallas_call(
        functools.partial(near_kernel, unroll, inner),
        out_shape=jax.ShapeDtypeStruct((slots, 128), F32),
        in_specs=[pl.BlockSpec(memory_space=pltpu.SMEM), vmem, vmem, vmem],
        out_specs=vmem,
        scratch_shapes=[
            pltpu.VMEM((slots, FEATURES, 128), BF16),
            pltpu.VMEM((slots, 128), F32),
            pltpu.VMEM((unroll, FEATURES * 8, 128), F32),
            pltpu.VMEM((FEATURES * 8, 128), F32),
            pltpu.VMEM((senders, cap, 128), F32),
            pltpu.SemaphoreType.DMA,
            pltpu.SemaphoreType.DMA,
        ],
        compiler_params=pltpu.CompilerParams(
            vmem_limit_bytes=28 << 20, collective_id=0, has_side_effects=True
        ),
        cost_estimate=pl.CostEstimate(
            flops=2 * slots * 512 * 128 * 256, bytes_accessed=8 << 20, transcendentals=slots << 17
        ),
        name="near_field",
    )(near_list, src, offsets, far)


def surface_weights():
    grid = np.linspace(-1.0, 1.0, ORDER)
    points = np.stack(np.meshgrid(grid, grid, grid, indexing="ij"), 0).reshape(3, -1)
    on_surface = np.max(np.abs(points), axis=0) > 1.0 - 1e-09
    points = (points[:, on_surface] * RADIUS).astype(np.float32)
    fill = 320 - points.shape[1]
    points = np.concatenate([points, np.repeat(points[:, :1], fill, axis=1)], axis=1)

    def split(v):
        high = v.astype(ml_dtypes.bfloat16).astype(np.float32)
        rest = v - high
        middle = rest.astype(ml_dtypes.bfloat16).astype(np.float32)
        return high, middle, rest - middle

    rows = []
    for c in range(3):
        h, m, l = split(-2.0 * points[c])
        rows += [h, m, l, h, m, h]
    rows += [np.ones(320, np.float32)] * 3
    rows += list(split(np.sum(points * points, axis=0)))
    rows += [np.zeros(320, np.float32)] * (FEATURES - len(rows))
    rows = np.stack(rows)
    main = np.repeat(rows[:, :256], 8, axis=0)
    last = np.zeros((FEATURES, 8, 512), np.float32)
    for s in range(8):
        last[:, s, 64 * s : 64 * s + 64] = rows[:, 256:]
    last = last.reshape(FEATURES * 8, 512)
    return main.astype(ml_dtypes.bfloat16), last.astype(ml_dtypes.bfloat16)


def far_kernel(unroll, dest, off, dens, main, last, out, tfeat, shift):
    ones = jnp.ones((8, 128), F32)
    zeros = jnp.zeros((8, 128), F32)
    out[...] = jnp.zeros_like(out)
    for u in range(unroll):
        for f in range(21, 24):
            tfeat[u, 8 * f : 8 * f + 8] = ones
        for f in range(24, FEATURES):
            tfeat[u, 8 * f : 8 * f + 8] = zeros
    row_of_lane = lax.broadcasted_iota(jnp.int32, (128, 8 * FEATURES), 1) % 8
    low_half = lax.broadcasted_iota(jnp.int32, (1, 128), 1) < 64

    def rows(i, carry):
        for u in range(unroll):
            first = (i * unroll + u) * 8
            at = [dest[first + t] for t in range(8)]
            for t in range(8):
                for c in range(3):
                    shift[u, c, t : t + 1, :] = off[at[t] // 8, c, pl.ds(at[t] % 8, 1), :]
            for f, v in enumerate(target_features(*(shift[u, c] for c in range(3)), 0.0)):
                tfeat[u, 8 * f : 8 * f + 8] = v
            turned = tfeat[u].astype(BF16).T
            weights = [dens[pl.ds(first + t, 1), :] for t in range(8)]
            tail_sq = jnp.dot(turned, last[...], preferred_element_type=F32)
            for p in range(4):
                pair = jnp.where(
                    low_half,
                    weights[2 * p][:, 256:384],
                    pltpu.roll(weights[2 * p + 1][:, 256:384], 64, 1),
                )
                tail = lax.rsqrt(tail_sq[:, 128 * p : 128 * p + 128]) * pair
                for h in range(2):
                    t = 2 * p + h
                    left = jnp.where(row_of_lane == t, turned, jnp.zeros_like(turned))
                    dist_sq = jnp.dot(left, main[...], preferred_element_type=F32)
                    total = lax.rsqrt(dist_sq[:, :128]) * weights[t][:, :128]
                    total = total + lax.rsqrt(dist_sq[:, 128:]) * weights[t][:, 128:256]
                    total = total + jnp.where(low_half == (h == 0), tail, 0.0)
                    line = jnp.sum(total.T, axis=0, keepdims=True)
                    out[pl.ds(at[t], 1), :] = line * (0.25 / (math.pi * HALF))
        return carry

    lax.fori_loop(0, dens.shape[0] // (8 * unroll), rows, 0)


def far_field(dest, offsets, dens, unroll=4):
    devices, _, cap, points = offsets.shape
    main, last = surface_weights()
    vmem = pl.BlockSpec(memory_space=pltpu.VMEM)
    return pl.pallas_call(
        functools.partial(far_kernel, unroll),
        out_shape=jax.ShapeDtypeStruct((devices * cap, points), F32),
        in_specs=[pl.BlockSpec(memory_space=pltpu.SMEM)] + [vmem] * 4,
        out_specs=vmem,
        scratch_shapes=[
            pltpu.VMEM((unroll, FEATURES * 8, 128), F32),
            pltpu.VMEM((unroll, 3, 8, 128), F32),
        ],
        compiler_params=pltpu.CompilerParams(vmem_limit_bytes=14 << 20),
        cost_estimate=pl.CostEstimate(
            flops=2 * dens.shape[0] * 128 * 256 * 384,
            bytes_accessed=4 << 20,
            transcendentals=dens.shape[0] * 128 * 320,
        ),
        name="far_field",
    )(dest, offsets, dens, jnp.asarray(main), jnp.asarray(last))


def on_device(
    parent_local,
    parent_slot,
    child_octant,
    child_m2l,
    l2l_ops,
    leaf_center,
    src_coords,
    src_charge,
    obs_owner,
    obs_offset,
    near_slots,
):
    devices = lax.axis_size(AXES)
    leaf_dev, width = child_m2l.shape
    slots, _, points = obs_offset.shape
    cap = slots // devices
    me = lax.axis_index(AXES)
    mine = lax.dynamic_slice_in_dim(obs_owner, me * leaf_dev, leaf_dev)

    rim = from_behind(parent_local[parent_local.shape[0] - RIM :], AXES, 1)
    packed, dest = pack(mine, jnp.transpose(src_coords, (1, 0, 2)), src_charge, leaf_center, devices, cap)

    offsets = jnp.transpose(obs_offset, (1, 0, 2))
    outgoing = jnp.transpose(offsets.reshape(3, devices, cap, points), (1, 0, 2, 3))
    outgoing, rim = lax.optimization_barrier((outgoing, rim))
    at_leaves = lax.all_to_all(outgoing, AXES, 0, 0, tiled=True)

    parents = jnp.concatenate([rim, parent_local], axis=0)
    moved = jnp.einsum("pr,oqr->opq", parents, l2l_ops, precision=lax.Precision.HIGHEST)
    stacked = moved.reshape(l2l_ops.shape[0] * parents.shape[0], width)
    which = child_octant * parents.shape[0] + parent_slot
    leaf_local, dens = leaf_rows(which, stacked, child_m2l, 384)
    packed, dens = lax.optimization_barrier((packed, dens))
    received = lax.all_to_all(packed, AXES, 0, 0, tiled=True)
    far = far_field(dest, at_leaves, dens)
    far = far.reshape(devices, cap, points)
    near_list = jnp.transpose(near_slots).reshape(-1)
    potential = near_field(received, offsets, near_list, far, lax.axis_size("dom"))
    return (leaf_local, potential)


def solution(mesh):
    placed = (
        P(AXES, None),
        P(AXES),
        P(AXES),
        P(AXES, None),
        P(),
        P(AXES, None),
        P(AXES, None, None),
        P(AXES, None),
        P(),
        P(AXES, None, None),
        P(AXES, None),
    )
    return jax.shard_map(
        on_device,
        mesh=mesh,
        in_specs=placed,
        out_specs=(P(AXES, None), P(AXES, None)),
        check_vma=False,
    )
```
